32 devices in a mesh: row: 4 (over y, core), col: 8 (over z, x).
Axes of the slice: x: 2, y: 2, z: 4, core: 2. Of those that a mesh axis runs over, the one named last changes fastest.
Arguments:
- positions: float32 [3, 16384], P(None, ('row', 'col')), may hold values from 0 to 4
- momenta: float32 [3, 16384], P(None, ('row', 'col')), may hold values from -6 to 6
- species: int32 [16384], P(('row', 'col')), may hold values from 0 to 1
- tile_a: int32 [4, 8, 256], P('row', 'col'), may hold values from 0 to 31, as said below
- tile_b: int32 [4, 8, 256], P('row', 'col'), may hold values from 0 to 15
- tile_count: int32 [4, 8], P('row', 'col'), may hold values from 1 to 256, as said below
Outputs:
- trial_positions: float32 [3, 16384], P(None, ('row', 'col'))
- trial_momenta: float32 [3, 16384], P(None, ('row', 'col'))
- end_force: float32 [3, 16384], P(None, ('row', 'col'))
The draws below stay inside these ranges and needn't reach their ends.
Inputs may be any that keep to these rules, and one draw needn't show every extreme that they name: Live slots of one grid cell name distinct (tile_a, tile_b) pairs; slots from tile_count on hold 0. `tile_count`: some grid cell of row 0 has exactly 256 live slots.
All inputs are finite; a program needn't handle non-finite values.
Results may differ from the reference program's by a relative error of at most 0.0003.
Values sent between devices are 32-bit elements; how exact they have to be, the bound alone decides.
A program may use at most 64 MiB of HBM per device.

```python
import jax
import jax.numpy as jnp
from jax import lax

TILE_DEV = 4
MAXP = 256
PARTICLES = 16384
N_ROW = 4
N_COL = 8


def pair_lists(key):
    key = jax.random.fold_in(key, 7)
    key_count, key_fill, key_perm = jax.random.split(key, 3)
    row_tiles = TILE_DEV * N_COL
    column_tiles = TILE_DEV * N_ROW
    rows = jnp.arange(N_ROW, dtype=jnp.int32)
    upper = MAXP * (1 + 3 * (N_ROW - 1 - rows)) // (1 + 3 * (N_ROW - 1))
    lower = jnp.maximum(upper // 2, 1)
    counts = jax.random.randint(key_count, (N_ROW, N_COL), lower[:, None], upper[:, None] + 1).astype(jnp.int32)
    filled = jax.random.randint(key_fill, (), 0, N_COL)
    counts = counts.at[0, filled].set(MAXP)
    device_keys = jax.random.split(key_perm, N_ROW * N_COL)
    orders = jax.vmap(lambda single: jax.random.permutation(single, row_tiles * column_tiles)[:MAXP])(device_keys)
    orders = orders.reshape(N_ROW, N_COL, MAXP).astype(jnp.int32)
    live = jnp.arange(MAXP, dtype=jnp.int32)[None, None, :] < counts[:, :, None]
    first = jnp.where(live, orders // column_tiles, 0).astype(jnp.int32)
    second = jnp.where(live, orders % column_tiles, 0).astype(jnp.int32)
    return (first, second, counts)


def draw_tile_a(key, part):
    return pair_lists(key)[0]


def draw_tile_b(key, part):
    return pair_lists(key)[1]


def draw_tile_count(key, part):
    return pair_lists(key)[2]


def set_ends(array, stream_key, smallest, largest):
    extent = array.shape
    spot = [jax.random.randint(jax.random.fold_in(stream_key, axis), (), 0, extent[axis]) for axis in range(len(extent))]
    array = array.at[tuple(spot)].set(smallest)
    longest = extent.index(max(extent))
    spot[longest] = (spot[longest] + 1) % extent[longest]
    return array.at[tuple(spot)].set(largest)


def block_scale(rng, dims, pieces, low, top_value):
    factor_of, own = 1.0, jax.random.fold_in(rng, 6)
    for position, shards_of in pieces:
        draws = jnp.exp(jax.random.uniform(jax.random.fold_in(own, position), (shards_of,), jnp.float32, low / len(pieces), top_value / len(pieces)))
        factor_of = factor_of * jnp.repeat(draws, dims[position] // shards_of).reshape([-1 if axis == position else 1 for axis in range(len(dims))])
    return factor_of


def normal_values(key, extent, spread, limit, cuts=(), kind=jnp.bfloat16):
    loudness = block_scale(key, extent, cuts, -0.22, 0.18) if cuts else 1.0
    entries = jax.random.normal(key, extent, jnp.float32) * spread * loudness
    return jnp.minimum(jnp.maximum(entries, -limit), limit).astype(kind)


def setup_inputs(seed: int = 0) -> dict:
    keys = jax.random.split(jax.random.key(seed), 7)
    positions = jnp.clip(4.0 * jax.random.uniform(keys[0], (3, PARTICLES), jnp.float32) ** block_scale(keys[0], (3, PARTICLES), ((1, 32),), -0.2, 0.2), 0.0, 4.0)
    momenta = normal_values(keys[1], (3, PARTICLES), 1.0, 6.0, ((1, 32),), jnp.float32)
    species = set_ends(jax.random.randint(keys[2], (PARTICLES,), 0, 2), jax.random.fold_in(keys[2], 1), 0, 1).astype(jnp.int32)
    tile_a = draw_tile_a(jax.random.fold_in(keys[6], 71), 0)
    tile_b = draw_tile_b(jax.random.fold_in(keys[6], 71), 0)
    tile_count = draw_tile_count(jax.random.fold_in(keys[6], 71), 0)
    return dict(positions=positions, momenta=momenta, species=species, tile_a=tile_a, tile_b=tile_b, tile_count=tile_count)


SCREENING = 1.0
SOFTENING = 0.25
GRAVITY = 0.5
LIGHT_CHARGE = 1.0
HEAVY_CHARGE = 2.5
HALF_STEP = 0.1
TIME_STEP = 0.2
tile_width = 128

def tile_pair_force(near, far, same):
    offset = near[:3, :, :, None] - far[:3, :, None, :]
    radius = jnp.sqrt(lax.optimization_barrier(jnp.sum(offset * offset, axis=0)) + SOFTENING)
    weight = near[3][:, :, None] * far[3][:, None, :] * jnp.exp(-SCREENING * radius) * (1.0 + SCREENING * radius) / (radius * radius * radius)
    diagonal = jnp.arange(tile_width)[:, None] == jnp.arange(tile_width)[None, :]
    weight = jnp.where(jnp.logical_and(same[:, None, None], diagonal[None]), 0.0, weight)
    return jnp.transpose(lax.optimization_barrier(jnp.sum(weight[None] * offset, axis=3)), (1, 0, 2))

def weight_of(mass):
    return jnp.zeros((3, mass.shape[0]), jnp.float32).at[2].set(-GRAVITY * mass)

def reference(positions, momenta, species, tile_a, tile_b, tile_count):
    charge = jnp.where(species == 1, HEAVY_CHARGE, LIGHT_CHARGE).astype(jnp.float32)
    total_tiles = positions.shape[1] // tile_width
    row_ids = jnp.arange(N_ROW, dtype=jnp.int32)[:, None, None]
    col_ids = jnp.arange(N_COL, dtype=jnp.int32)[None, :, None]
    firsts = (row_ids * N_COL * TILE_DEV + tile_a).astype(jnp.int32).reshape(-1, MAXP)
    seconds = ((tile_b // TILE_DEV * N_COL + col_ids) * TILE_DEV + tile_b % TILE_DEV).astype(jnp.int32).reshape(-1, MAXP)
    live = (jnp.arange(MAXP, dtype=jnp.int32)[None, None, :] < tile_count[:, :, None]).reshape(-1, MAXP)
    gravity = weight_of(charge)

    def forces(places):
        state = jnp.concatenate([places, charge[None]], axis=0).reshape(4, total_tiles, tile_width)

        def visit(total, block):
            first, second, alive = block
            term = tile_pair_force(state[:, first], state[:, second], first == second)
            term = term * alive.astype(jnp.float32)[:, None, None]
            return (total.at[first].add(term), None)
        total, _ = lax.scan(visit, jnp.zeros((total_tiles, 3, tile_width), jnp.float32), (firsts, seconds, live))
        return jnp.transpose(total, (1, 0, 2)).reshape(3, -1) + gravity
    start_force = forces(positions)
    half = momenta + HALF_STEP * start_force
    moved = positions + TIME_STEP * half / charge
    end_force = forces(moved)
    ahead = half + HALF_STEP * end_force
    return (moved, ahead, end_force)
```

```python
import functools
import math

import jax
import jax.numpy as jnp
from jax import lax
from jax.experimental import pallas as pl
from jax.experimental.pallas import tpu as pltpu
from jax.sharding import PartitionSpec as P

SOFTENING = 0.25
GRAVITY = 0.5
LIGHT_CHARGE = 1.0
HEAVY_CHARGE = 2.5
HALF_STEP = 0.1
TIME_STEP = 0.2
tile_width = 128
scale = 1.0 / math.log(2.0)
middle = 2.0
depth = 32
MESH = pl.DeviceIdType.MESH
f32, bf16 = jnp.float32, jnp.bfloat16


def peers(axes, name):
    me, size = lax.axis_index(name), axes[name]
    return [{name: lax.rem(me + step, size)} for step in range(1, size)]


def remote(source, target, sems, which, peer):
    return pltpu.make_async_remote_copy(
        src_ref=source,
        dst_ref=target,
        send_sem=sems.at[0, which],
        recv_sem=sems.at[1, which],
        device_id=peer,
        device_id_type=MESH,
    )


def charge_of(species):
    return jnp.where(species == 1, HEAVY_CHARGE, LIGHT_CHARGE).astype(f32)


def pack(packed, places, charge, tiles):
    for tile in range(tiles):
        lanes = slice(tile * tile_width, (tile + 1) * tile_width)
        packed[4 * tile : 4 * tile + 3, :] = places[:, lanes]
        packed[4 * tile + 3 : 4 * tile + 4, :] = charge[:, lanes]


def pieces(value, number):
    parts = []
    for _ in range(number - 1):
        part = value.astype(bf16).astype(f32)
        parts.append(part)
        value = value - part
    parts.append(value.astype(bf16).astype(f32))
    return parts


pairs_of_pieces = ((0, 0), (0, 1), (1, 0), (0, 2), (2, 0), (1, 1))


def flat(ref):
    return ref.reshape(ref.shape[0] * ref.shape[1], ref.shape[2])


def component(ref, start, index, count):
    return ref[pl.ds(4 * start + index, count, stride=4), :]


def prepare_near(rows, near_f, near):
    for start in range(0, near.shape[0], 8):
        here = pl.ds(start, 8)
        square = 0.0
        for axis in range(3):
            value = (component(rows, start, axis, 8) - middle) * scale
            square = square + value * value
            split = pieces(value, 3)
            for row, (left, _) in enumerate(pairs_of_pieces):
                near_f[here, 6 * axis + row, :] = -2.0 * split[left]
        for row, piece in enumerate(pieces(square, 3)):
            near_f[here, 18 + row, :] = piece
            near_f[here, 21 + row, :] = jnp.ones_like(piece)
    near[...] = near_f[...].astype(bf16)


def prepare_far(cols, far_f, far, load_f, load):
    tiles = far.shape[0]
    for start in range(0, tiles, 8):
        here = pl.ds(start, 8)
        charge = component(cols, start, 3, 8)
        square = SOFTENING * scale * scale
        for axis in range(3):
            value = (component(cols, start, axis, 8) - middle) * scale
            square = square + value * value
            split = pieces(value, 3)
            for row, (_, right) in enumerate(pairs_of_pieces):
                far_f[here, 6 * axis + row, :] = split[right]
            for row, piece in enumerate(pieces(charge * value, 2)):
                load_f[here, 4 * row + axis, :] = piece
        load_f[here, 3, :] = charge
        for row, piece in enumerate(pieces(square, 3)):
            far_f[here, 18 + row, :] = jnp.ones_like(piece)
            far_f[here, 21 + row, :] = piece
    for tile in range(tiles):
        far[tile] = far_f[tile].T.astype(bf16)
    single = load_f[...].astype(bf16)
    load[:, :, :tile_width] = single
    load[:, :, tile_width:] = single


def visit_pairs(lists, near, far, load, terms):
    slots = lists.shape[1]
    unroll = math.gcd(slots, 64)

    def visit(step, carry):
        for index in range(unroll):
            slot = step * unroll + index
            first, second = lists[0, slot], lists[1, slot]
            square = jnp.dot(far[second], near[first], preferred_element_type=f32)
            square = jnp.maximum(square, SOFTENING * scale * scale)
            inverse = lax.rsqrt(square)
            decay = jnp.exp2(-(square * inverse))
            weight = decay * (inverse * inverse) * (inverse + 1.0 / scale)
            high = weight.astype(bf16)
            low = (weight - high.astype(f32)).astype(bf16)
            both = jnp.concatenate([high, low], axis=0)
            term = jnp.dot(load[second], both, preferred_element_type=f32)
            terms[pl.ds(pl.multiple_of(8 * slot, 8), 8), :] = term[:8]
        return carry

    lax.fori_loop(0, slots // unroll, visit, 0)


def combine(chosen, terms, partial):
    slots = chosen.shape[1]
    tiles = chosen.shape[0]

    def row(index):
        return terms[pl.ds(index, slots, stride=8), :]

    for part in range(4):
        value = row(part) if part == 3 else row(part) + row(4 + part)
        high = value.astype(bf16)
        low = (value - high.astype(f32)).astype(bf16)
        both = jnp.dot(chosen, jnp.concatenate([high, low], axis=1), preferred_element_type=f32)
        partial[pl.ds(part, tiles, stride=4), :] = both[:, :tile_width] + both[:, tile_width:]


def step_kernel(
    axes, tiles, pos_ref, mom_ref, spec_ref, first_ref, count_ref, lists_hbm,
    moved_ref, ahead_ref, end_ref,
    lists, packed_a, packed_b, rows_a, rows_b, cols_a, cols_b, partial_a, partial_b, arrived_a, arrived_b,
    near_f, near, far_f, far, load_f, load, terms, chosen,
    spread_a, spread_b, reduce_a, reduce_b, list_sem,
):
    my_row, my_col = lax.axis_index("row"), lax.axis_index("col")
    across_col, across_row = peers(axes, "col"), peers(axes, "row")
    barrier = pltpu.get_barrier_semaphore()
    for peer in across_col + across_row:
        pl.semaphore_signal(barrier, inc=1, device_id=peer, device_id_type=MESH)
    fetch = pltpu.make_async_copy(lists_hbm, lists, list_sem)
    fetch.start()
    charge = charge_of(spec_ref[...])
    pack(packed_a, pos_ref[...], charge, tiles)
    pl.semaphore_wait(barrier, len(across_col + across_row))

    def spread(packed, rows_ref, cols_ref, sems):
        mine, level = rows_ref.at[my_col], cols_ref.at[my_row]
        jobs = [(mine, peer) for peer in across_col] + [(level, peer) for peer in across_row]
        copies = [remote(packed, target, sems, which, peer) for which, (target, peer) in enumerate(jobs)]
        for copy in copies:
            copy.start()
        rows_ref[my_col] = packed[...]
        cols_ref[my_row] = packed[...]
        return copies

    def collect(partial, arrived, sems):
        copies = [
            remote(partial.at[peer["col"]], arrived.at[my_col], sems, which, peer)
            for which, peer in enumerate(across_col)
        ]
        for copy in copies:
            copy.start()
        arrived[my_col] = partial[my_col]
        for copy in copies:
            copy.wait()
        total = arrived[0]
        for index in range(1, axes["col"]):
            total = total + arrived[index]
        return total

    def evaluate(packed, rows_ref, cols_ref, spread_sems, partial, arrived, sems, places, meanwhile=lambda: None):
        copies = spread(packed, rows_ref, cols_ref, spread_sems)
        meanwhile()
        for copy in copies:
            copy.wait()
        prepare_near(flat(rows_ref), near_f, near)
        prepare_far(flat(cols_ref), far_f, far, load_f, load)
        visit_pairs(lists, near, far, load, terms)
        combine(chosen[...], terms, flat(partial))
        total = collect(partial, arrived, sems)
        moment = jnp.concatenate([total[4 * tile : 4 * tile + 3, :] for tile in range(tiles)], axis=1)
        weights = jnp.concatenate([total[4 * tile + 3 : 4 * tile + 4, :] for tile in range(tiles)], axis=1)
        third = lax.broadcasted_iota(jnp.int32, moment.shape, 0) == 2
        force = (charge * (scale * scale)) * ((places - middle) * scale * weights - moment)
        return force + jnp.where(third, -GRAVITY * charge, 0.0)

    def meanwhile():
        near_f[...] = jnp.zeros_like(near_f)
        far_f[...] = jnp.zeros_like(far_f)
        load_f[...] = jnp.zeros_like(load_f)
        tile = lax.broadcasted_iota(jnp.int32, chosen.shape, 0)
        slot = lax.broadcasted_iota(jnp.int32, chosen.shape, 1)
        live = (tile == first_ref[...]) & (slot < count_ref[...])
        chosen[...] = jnp.where(live, 1.0, 0.0).astype(bf16)
        fetch.wait()

    places = pos_ref[...]
    force = evaluate(packed_a, rows_a, cols_a, spread_a, partial_a, arrived_a, reduce_a, places, meanwhile)
    half = mom_ref[...] + HALF_STEP * force
    moved = places + TIME_STEP * half / charge
    moved_ref[...] = moved
    pack(packed_b, moved, charge, tiles)
    force = evaluate(packed_b, rows_b, cols_b, spread_b, partial_b, arrived_b, reduce_b, moved)
    ahead_ref[...] = half + HALF_STEP * force
    end_ref[...] = force


def per_device(row_count, col_count, positions, momenta, species, tile_a, tile_b, tile_count):
    own = positions.shape[1]
    tiles = own // tile_width
    axes = {"col": col_count, "row": row_count}
    vmem = pl.BlockSpec(memory_space=pltpu.VMEM)
    anywhere = pl.BlockSpec(memory_space=pl.ANY)
    slots = tile_a.shape[-1]
    firsts = tile_a.reshape(1, slots)
    lists = jnp.concatenate([firsts, tile_b.reshape(1, slots)], axis=0)
    block = (4 * tiles, tile_width)
    near_count, far_count = col_count * tiles, row_count * tiles
    own_shape = jax.ShapeDtypeStruct((3, own), f32)
    spreads = pltpu.SemaphoreType.DMA((2, col_count + row_count - 2))
    reduces = pltpu.SemaphoreType.DMA((2, col_count - 1))
    rows, cols = pltpu.VMEM((col_count,) + block, f32), pltpu.VMEM((row_count,) + block, f32)
    return tuple(
        pl.pallas_call(
            functools.partial(step_kernel, axes, tiles),
            out_shape=(own_shape,) * 3,
            in_specs=[vmem] * 5 + [anywhere],
            out_specs=(vmem,) * 3,
            scratch_shapes=[
                pltpu.SMEM((2, slots), jnp.int32),
                pltpu.VMEM(block, f32), pltpu.VMEM(block, f32),
                rows, rows, cols, cols, rows, rows, rows, rows,
                pltpu.VMEM((near_count, depth, tile_width), f32),
                pltpu.VMEM((near_count, depth, tile_width), bf16),
                pltpu.VMEM((far_count, depth, tile_width), f32),
                pltpu.VMEM((far_count, tile_width, depth), bf16),
                pltpu.VMEM((far_count, 16, tile_width), f32),
                pltpu.VMEM((far_count, 16, 2 * tile_width), bf16),
                pltpu.VMEM((8 * slots, tile_width), f32),
                pltpu.VMEM((near_count, slots), bf16),
                spreads, spreads, reduces, reduces, pltpu.SemaphoreType.DMA,
            ],
            compiler_params=pltpu.CompilerParams(collective_id=0, has_side_effects=True, vmem_limit_bytes=48 * 2**20),
            name="step",
        )(positions, momenta, species.reshape(1, own), firsts, tile_count, lists)
    )


def solution(mesh):
    in_specs = (
        P(None, ("row", "col")),
        P(None, ("row", "col")),
        P(("row", "col")),
        P("row", "col", None),
        P("row", "col", None),
        P("row", "col"),
    )
    out_specs = (P(None, ("row", "col")), P(None, ("row", "col")), P(None, ("row", "col")))
    body = functools.partial(per_device, mesh.shape["row"], mesh.shape["col"])
    return jax.shard_map(body, mesh=mesh, in_specs=in_specs, out_specs=out_specs, check_vma=False)
```

```python
import functools
import math

import jax
import jax.numpy as jnp
from jax import lax
from jax.experimental import pallas as pl
from jax.experimental.pallas import tpu as pltpu
from jax.sharding import PartitionSpec as P

SOFTENING = 0.25
GRAVITY = 0.5
LIGHT_CHARGE = 1.0
HEAVY_CHARGE = 2.5
HALF_STEP = 0.1
TIME_STEP = 0.2
tile_width = 128
scale = 1.0 / math.log(2.0)
middle = 2.0
depth = 32
longest = 128
grant = 48 * 2**20
MESH = pl.DeviceIdType.MESH
f32, bf16 = jnp.float32, jnp.bfloat16


def peers(axes, name):
    me, size = lax.axis_index(name), axes[name]
    return [{name: lax.rem(me + step, size)} for step in range(1, size)]


def remote(source, target, sems, which, peer):
    return pltpu.make_async_remote_copy(
        src_ref=source,
        dst_ref=target,
        send_sem=sems.at[0, which],
        recv_sem=sems.at[1, which],
        device_id=peer,
        device_id_type=MESH,
    )


def charge_of(species):
    return jnp.where(species == 1, HEAVY_CHARGE, LIGHT_CHARGE).astype(f32)


def pack(packed, places, charge, tiles):
    for tile in range(tiles):
        lanes = slice(tile * tile_width, (tile + 1) * tile_width)
        packed[4 * tile : 4 * tile + 3, :] = places[:, lanes]
        packed[4 * tile + 3 : 4 * tile + 4, :] = charge[:, lanes]


def pieces(value, number):
    parts = []
    for _ in range(number - 1):
        part = value.astype(bf16).astype(f32)
        parts.append(part)
        value = value - part
    parts.append(value.astype(bf16).astype(f32))
    return parts


pairs_of_pieces = ((0, 0), (0, 1), (1, 0), (0, 2), (2, 0), (1, 1))


def flat(ref):
    return ref.reshape(ref.shape[0] * ref.shape[1], ref.shape[2])


def component(ref, start, index, count):
    return ref[pl.ds(4 * start + index, count, stride=4), :]


def prepare_near(rows, near_f, near):
    for start in range(0, near.shape[0], 8):
        here = pl.ds(start, 8)
        square = 0.0
        for axis in range(3):
            value = (component(rows, start, axis, 8) - middle) * scale
            square = square + value * value
            split = pieces(value, 3)
            for row, (left, _) in enumerate(pairs_of_pieces):
                near_f[here, 6 * axis + row, :] = -2.0 * split[left]
        for row, piece in enumerate(pieces(square, 3)):
            near_f[here, 18 + row, :] = piece
            near_f[here, 21 + row, :] = jnp.ones_like(piece)
    near[...] = near_f[...].astype(bf16)


def prepare_far(cols, far_f, far, load_f, load):
    tiles = far.shape[0]
    for start in range(0, tiles, 8):
        here = pl.ds(start, 8)
        charge = component(cols, start, 3, 8)
        square = SOFTENING * scale * scale
        for axis in range(3):
            value = (component(cols, start, axis, 8) - middle) * scale
            square = square + value * value
            split = pieces(value, 3)
            for row, (_, right) in enumerate(pairs_of_pieces):
                far_f[here, 6 * axis + row, :] = split[right]
            for row, piece in enumerate(pieces(charge * value, 2)):
                load_f[here, 4 * row + axis, :] = piece
        load_f[here, 3, :] = charge
        for row, piece in enumerate(pieces(square, 3)):
            far_f[here, 18 + row, :] = jnp.ones_like(piece)
            far_f[here, 21 + row, :] = piece
    for tile in range(tiles):
        far[tile] = far_f[tile].T.astype(bf16)
    single = load_f[...].astype(bf16)
    load[:, :, :tile_width] = single
    load[:, :, tile_width:] = single


def visit_pairs(firsts, seconds, near, far, load, terms):
    slots = firsts.shape[1]
    unroll = math.gcd(slots, longest)

    def visit(step, carry):
        for index in range(unroll):
            slot = step * unroll + index
            first, second = firsts[0, slot], seconds[0, slot]
            square = jnp.dot(far[second], near[first], preferred_element_type=f32)
            inverse = lax.rsqrt(square)
            decay = jnp.exp2(-(square * inverse))
            weight = decay * (inverse * inverse) * (inverse + 1.0 / scale)
            high = weight.astype(bf16)
            low = (weight - high.astype(f32)).astype(bf16)
            both = jnp.concatenate([high, low], axis=0)
            term = jnp.dot(load[second], both, preferred_element_type=f32)
            terms[pl.ds(pl.multiple_of(8 * slot, 8), 8), :] = term[:8]
        return carry

    lax.fori_loop(0, slots // unroll, visit, 0)


def combine(chosen, terms, partial):
    slots = chosen.shape[1]
    tiles = chosen.shape[0]

    def row(index):
        return terms[pl.ds(index, slots, stride=8), :]

    for part in range(4):
        value = row(part) if part == 3 else row(part) + row(4 + part)
        high = value.astype(bf16)
        low = (value - high.astype(f32)).astype(bf16)
        both = jnp.dot(chosen, jnp.concatenate([high, low], axis=1), preferred_element_type=f32)
        partial[pl.ds(part, tiles, stride=4), :] = both[:, :tile_width] + both[:, tile_width:]


def step_kernel(
    axes, tiles, pos_hbm, mom_hbm, spec_hbm, first_hbm, second_hbm, count,
    moved_ref, ahead_ref, end_ref,
    pos_ref, mom_ref, spec_ref, first_ref, firsts, seconds,
    packed_a, packed_b, rows_a, rows_b, cols_a, cols_b, partial_a, partial_b, arrived_a, arrived_b,
    near_f, near, far_f, far, load_f, load, terms, chosen,
    spread_a, spread_b, reduce_a, reduce_b, fetch_sems,
):
    my_row, my_col = lax.axis_index("row"), lax.axis_index("col")
    across_col, across_row = peers(axes, "col"), peers(axes, "row")
    barrier = pltpu.get_barrier_semaphore()
    for peer in across_col + across_row:
        pl.semaphore_signal(barrier, inc=1, device_id=peer, device_id_type=MESH)
    moves = (
        (pos_hbm, pos_ref), (spec_hbm, spec_ref), (second_hbm, seconds), (first_hbm, firsts),
        (first_hbm, first_ref), (mom_hbm, mom_ref),
    )
    fetches = [pltpu.make_async_copy(source, target, fetch_sems.at[which]) for which, (source, target) in enumerate(moves)]
    for fetch in fetches:
        fetch.start()
    for fetch in fetches[:2]:
        fetch.wait()
    charge = charge_of(spec_ref[...])
    pack(packed_a, pos_ref[...], charge, tiles)
    pl.semaphore_wait(barrier, len(across_col + across_row))

    def spread(packed, rows_ref, cols_ref, sems):
        mine, level = rows_ref.at[my_col], cols_ref.at[my_row]
        jobs = [(mine, peer) for peer in across_col] + [(level, peer) for peer in across_row]
        copies = [remote(packed, target, sems, which, peer) for which, (target, peer) in enumerate(jobs)]
        for copy in copies:
            copy.start()
        rows_ref[my_col] = packed[...]
        cols_ref[my_row] = packed[...]
        return copies

    def collect(partial, arrived, sems):
        copies = [
            remote(partial.at[peer["col"]], arrived.at[my_col], sems, which, peer)
            for which, peer in enumerate(across_col)
        ]
        for copy in copies:
            copy.start()
        arrived[my_col] = partial[my_col]
        for copy in copies:
            copy.wait()
        total = arrived[0]
        for index in range(1, axes["col"]):
            total = total + arrived[index]
        return total

    def evaluate(packed, rows_ref, cols_ref, spread_sems, partial, arrived, sems, places, meanwhile=lambda: None):
        copies = spread(packed, rows_ref, cols_ref, spread_sems)
        meanwhile()
        for copy in copies:
            copy.wait()
        prepare_near(flat(rows_ref), near_f, near)
        prepare_far(flat(cols_ref), far_f, far, load_f, load)
        visit_pairs(firsts, seconds, near, far, load, terms)
        combine(chosen[...], terms, flat(partial))
        total = collect(partial, arrived, sems)
        moment = jnp.concatenate([total[4 * tile : 4 * tile + 3, :] for tile in range(tiles)], axis=1)
        weights = jnp.concatenate([total[4 * tile + 3 : 4 * tile + 4, :] for tile in range(tiles)], axis=1)
        third = lax.broadcasted_iota(jnp.int32, moment.shape, 0) == 2
        force = (charge * (scale * scale)) * ((places - middle) * scale * weights - moment)
        return force + jnp.where(third, -GRAVITY * charge, 0.0)

    def meanwhile():
        near_f[...] = jnp.zeros_like(near_f)
        far_f[...] = jnp.zeros_like(far_f)
        load_f[...] = jnp.zeros_like(load_f)
        for fetch in fetches[2:]:
            fetch.wait()
        tile = lax.broadcasted_iota(jnp.int32, chosen.shape, 0)
        slot = lax.broadcasted_iota(jnp.int32, chosen.shape, 1)
        live = (tile == first_ref[...]) & (slot < count[0, 0])
        chosen[...] = jnp.where(live, 1.0, 0.0).astype(bf16)

    places = pos_ref[...]
    force = evaluate(packed_a, rows_a, cols_a, spread_a, partial_a, arrived_a, reduce_a, places, meanwhile)
    half = mom_ref[...] + HALF_STEP * force
    moved = places + TIME_STEP * half / charge
    moved_ref[...] = moved
    pack(packed_b, moved, charge, tiles)
    force = evaluate(packed_b, rows_b, cols_b, spread_b, partial_b, arrived_b, reduce_b, moved)
    ahead_ref[...] = half + HALF_STEP * force
    end_ref[...] = force


def finish_kernel(moved_ref, ahead_ref, end_ref, trial_ref, momenta_ref, force_ref, sems):
    moves = ((moved_ref, trial_ref), (ahead_ref, momenta_ref), (end_ref, force_ref))
    copies = [pltpu.make_async_copy(source, target, sems.at[which]) for which, (source, target) in enumerate(moves)]
    for copy in copies:
        copy.start()
    for copy in copies:
        copy.wait()


def per_device(row_count, col_count, positions, momenta, species, tile_a, tile_b, tile_count):
    own = positions.shape[1]
    tiles = own // tile_width
    axes = {"col": col_count, "row": row_count}
    vmem = pl.BlockSpec(memory_space=pltpu.VMEM)
    hbm = pl.BlockSpec(memory_space=pltpu.HBM)
    slots = tile_a.shape[-1]
    block = (4 * tiles, tile_width)
    near_count, far_count = col_count * tiles, row_count * tiles
    own_shape = jax.ShapeDtypeStruct((3, own), f32)
    spreads = pltpu.SemaphoreType.DMA((2, col_count + row_count - 2))
    reduces = pltpu.SemaphoreType.DMA((2, col_count - 1))
    rows, cols = pltpu.VMEM((col_count,) + block, f32), pltpu.VMEM((row_count,) + block, f32)
    outs = pl.pallas_call(
        functools.partial(step_kernel, axes, tiles),
        out_shape=(own_shape,) * 3,
        in_specs=[hbm] * 5 + [pl.BlockSpec(memory_space=pltpu.SMEM)],
        out_specs=(vmem,) * 3,
        scratch_shapes=[
            pltpu.VMEM((3, own), f32), pltpu.VMEM((3, own), f32), pltpu.VMEM((1, own), jnp.int32),
            pltpu.VMEM((1, slots), jnp.int32), pltpu.SMEM((1, slots), jnp.int32), pltpu.SMEM((1, slots), jnp.int32),
            pltpu.VMEM(block, f32), pltpu.VMEM(block, f32),
            rows, rows, cols, cols, rows, rows, rows, rows,
            pltpu.VMEM((near_count, depth, tile_width), f32),
            pltpu.VMEM((near_count, depth, tile_width), bf16),
            pltpu.VMEM((far_count, depth, tile_width), f32),
            pltpu.VMEM((far_count, tile_width, depth), bf16),
            pltpu.VMEM((far_count, 16, tile_width), f32),
            pltpu.VMEM((far_count, 16, 2 * tile_width), bf16),
            pltpu.VMEM((8 * slots, tile_width), f32),
            pltpu.VMEM((near_count, slots), bf16),
            spreads, spreads, reduces, reduces, pltpu.SemaphoreType.DMA((6,)),
        ],
        compiler_params=pltpu.CompilerParams(collective_id=0, has_side_effects=True, vmem_limit_bytes=grant),
        name="step",
    )(
        *(
            pltpu.with_memory_space_constraint(array, pltpu.HBM)
            for array in (
                positions, momenta, species.reshape(1, own),
                tile_a.reshape(1, slots), tile_b.reshape(1, slots),
            )
        ),
        tile_count,
    )
    return tuple(
        pl.pallas_call(
            finish_kernel,
            out_shape=(own_shape,) * 3,
            in_specs=[vmem] * 3,
            out_specs=(hbm,) * 3,
            scratch_shapes=[pltpu.SemaphoreType.DMA((3,))],
            compiler_params=pltpu.CompilerParams(vmem_limit_bytes=grant),
            name="finish",
        )(*outs)
    )


def solution(mesh):
    in_specs = (
        P(None, ("row", "col")),
        P(None, ("row", "col")),
        P(("row", "col")),
        P("row", "col", None),
        P("row", "col", None),
        P("row", "col"),
    )
    out_specs = (P(None, ("row", "col")), P(None, ("row", "col")), P(None, ("row", "col")))
    body = functools.partial(per_device, mesh.shape["row"], mesh.shape["col"])
    return jax.shard_map(body, mesh=mesh, in_specs=in_specs, out_specs=out_specs, check_vma=False)
```

```python
import functools
import math

import jax
import jax.numpy as jnp
from jax import lax
from jax.experimental import pallas as pl
from jax.experimental.pallas import tpu as pltpu
from jax.sharding import PartitionSpec as P

SOFTENING = 0.25
GRAVITY = 0.5
LIGHT_CHARGE = 1.0
HEAVY_CHARGE = 2.5
HALF_STEP = 0.1
TIME_STEP = 0.2
tile_width = 128
scale = 1.0 / math.log(2.0)
middle = 2.0
depth = 32
longest = 256
ahead = 8
grant = 48 * 2**20
MESH = pl.DeviceIdType.MESH
f32, bf16 = jnp.float32, jnp.bfloat16


def peers(axes, name):
    me, size = lax.axis_index(name), axes[name]
    return [{name: lax.rem(me + step, size)} for step in range(1, size)]


def remote(source, target, sems, which, peer):
    return pltpu.make_async_remote_copy(
        src_ref=source,
        dst_ref=target,
        send_sem=sems.at[0, which],
        recv_sem=sems.at[1, which],
        device_id=peer,
        device_id_type=MESH,
    )


def charge_of(species):
    return jnp.where(species == 1, HEAVY_CHARGE, LIGHT_CHARGE).astype(f32)


def pieces(value, number):
    parts = []
    for _ in range(number - 1):
        part = value.astype(bf16).astype(f32)
        parts.append(part)
        value = value - part
    parts.append(value.astype(bf16).astype(f32))
    return parts


pairs_of_pieces = ((0, 0), (0, 1), (1, 0), (0, 2), (2, 0), (1, 1))


def component(ref, start, index, count):
    return ref[pl.ds(start + index, count, stride=4), :]


def prepare_near(rows, base, near_f, near):
    for start in range(0, near.shape[0], 8):
        here = pl.ds(start, 8)
        square = 0.0
        for axis in range(3):
            value = (component(rows, base + 4 * start, axis, 8) - middle) * scale
            square = square + value * value
            split = pieces(value, 3)
            for row, (left, _) in enumerate(pairs_of_pieces):
                near_f[here, 6 * axis + row, :] = -2.0 * split[left]
        for row, piece in enumerate(pieces(square, 3)):
            near_f[here, 18 + row, :] = piece
            near_f[here, 21 + row, :] = jnp.ones_like(piece)
    single = near_f[...].astype(bf16)
    near[:, :, :tile_width] = single
    near[:, :, tile_width:] = -single


def prepare_far(cols, base, far_f, far, load_f, load):
    tiles = far.shape[0]
    for start in range(0, tiles, 8):
        here = pl.ds(start, 8)
        charge = component(cols, base + 4 * start, 3, 8)
        square = SOFTENING * scale * scale
        for axis in range(3):
            value = (component(cols, base + 4 * start, axis, 8) - middle) * scale
            square = square + value * value
            split = pieces(value, 3)
            for row, (_, right) in enumerate(pairs_of_pieces):
                far_f[here, 6 * axis + row, :] = split[right]
            for row, piece in enumerate(pieces(charge * value, 2)):
                load_f[here, 4 * row + axis, :] = piece
        load_f[here, 3, :] = charge
        for row, piece in enumerate(pieces(square, 3)):
            far_f[here, 18 + row, :] = jnp.ones_like(piece)
            far_f[here, 21 + row, :] = piece
    for tile in range(tiles):
        far[tile] = far_f[tile].T.astype(bf16)
    single = load_f[...].astype(bf16)
    load[:, :, :tile_width] = single
    load[:, :, tile_width:] = single


def visit_pairs(firsts, seconds, near, far, load, terms):
    slots = firsts.shape[1]
    unroll = math.gcd(slots, longest)

    def squares(slot):
        both = jnp.dot(far[seconds[0, slot]], near[firsts[0, slot]], preferred_element_type=f32)
        return both[:, :tile_width], both[:, tile_width:]

    def visit(step, carry):
        start = step * unroll
        ready = [squares(start + index) for index in range(ahead)]
        for index in range(unroll):
            slot = start + index
            square, negative = ready[index]
            if index + ahead < unroll:
                ready.append(squares(slot + ahead))
            inverse = lax.rsqrt(square)
            decay = jnp.exp2(negative * inverse)
            weight = decay * (inverse * inverse) * (inverse + 1.0 / scale)
            high = weight.astype(bf16)
            low = (weight - high.astype(f32)).astype(bf16)
            both = jnp.concatenate([high, low], axis=0)
            term = jnp.dot(load[seconds[0, slot]], both, preferred_element_type=f32)
            terms[pl.ds(pl.multiple_of(8 * slot, 8), 8), :] = term[:8]
        return carry

    lax.fori_loop(0, slots // unroll, visit, 0)


def combine(chosen, terms, partial, base):
    slots = chosen.shape[1]
    tiles = chosen.shape[0]

    def row(index):
        return terms[pl.ds(index, slots, stride=8), :]

    for part in range(4):
        value = row(part) if part == 3 else row(part) + row(4 + part)
        high = value.astype(bf16)
        low = (value - high.astype(f32)).astype(bf16)
        both = jnp.dot(chosen, jnp.concatenate([high, low], axis=1), preferred_element_type=f32)
        partial[pl.ds(base + part, tiles, stride=4), :] = both[:, :tile_width] + both[:, tile_width:]


def step_kernel(
    axes, tiles, pos_hbm, mom_hbm, spec_hbm, first_hbm, second_hbm, count,
    moved_ref, ahead_ref, end_ref,
    spec_ref, first_ref, firsts, seconds,
    packed, rows, cols, partial, arrived,
    near_f, near, far_f, far, load_f, load, terms, chosen,
    spread_sems, reduce_sems, fetch_sems,
):
    my_row, my_col = lax.axis_index("row"), lax.axis_index("col")
    across_col, across_row = peers(axes, "col"), peers(axes, "row")
    height = 4 * tiles
    barrier = pltpu.get_barrier_semaphore()
    for peer in across_col + across_row:
        pl.semaphore_signal(barrier, inc=1, device_id=peer, device_id_type=MESH)
    moves = (
        (pos_hbm, moved_ref), (spec_hbm, spec_ref), (second_hbm, seconds), (first_hbm, firsts),
        (first_hbm, first_ref), (mom_hbm, ahead_ref),
    )
    fetches = [pltpu.make_async_copy(source, target, fetch_sems.at[which]) for which, (source, target) in enumerate(moves)]
    for fetch in fetches:
        fetch.start()
    for fetch in fetches[:2]:
        fetch.wait()

    def pack(turn):
        places, charge = moved_ref[...], charge_of(spec_ref[...])
        for tile in range(tiles):
            lanes = slice(tile * tile_width, (tile + 1) * tile_width)
            packed[turn, 4 * tile : 4 * tile + 3, :] = places[:, lanes]
            packed[turn, 4 * tile + 3 : 4 * tile + 4, :] = charge[:, lanes]

    def block(turn, size, index):
        return pl.ds(pl.multiple_of((turn * size + index) * height, height), height)

    def prepare_lists():
        near_f[...] = jnp.zeros_like(near_f)
        far_f[...] = jnp.zeros_like(far_f)
        load_f[...] = jnp.zeros_like(load_f)
        for fetch in fetches[2:]:
            fetch.wait()
        tile = lax.broadcasted_iota(jnp.int32, chosen.shape, 0)
        slot = lax.broadcasted_iota(jnp.int32, chosen.shape, 1)
        live = (tile == first_ref[...]) & (slot < count[0, 0])
        chosen[...] = jnp.where(live, 1.0, 0.0).astype(bf16)

    pack(0)
    pl.semaphore_wait(barrier, len(across_col + across_row))

    def evaluate(turn, carry):
        mine, level = block(turn, axes["col"], my_col), block(turn, axes["row"], my_row)
        sems = spread_sems.at[turn]
        jobs = [(rows.at[mine], peer) for peer in across_col] + [(cols.at[level], peer) for peer in across_row]
        copies = [remote(packed.at[turn], target, sems, which, peer) for which, (target, peer) in enumerate(jobs)]
        for copy in copies:
            copy.start()
        rows[mine] = packed[turn]
        cols[level] = packed[turn]
        pl.when(turn == 0)(prepare_lists)
        for copy in copies:
            copy.wait()
        base = turn * axes["col"] * height
        prepare_near(rows, base, near_f, near)
        prepare_far(cols, turn * axes["row"] * height, far_f, far, load_f, load)
        visit_pairs(firsts, seconds, near, far, load, terms)
        combine(chosen[...], terms, partial, base)
        sems = reduce_sems.at[turn]
        copies = [
            remote(partial.at[block(turn, axes["col"], peer["col"])], arrived.at[mine], sems, which, peer)
            for which, peer in enumerate(across_col)
        ]
        for copy in copies:
            copy.start()
        arrived[mine] = partial[mine]
        for copy in copies:
            copy.wait()
        total = arrived[block(turn, axes["col"], 0)]
        for index in range(1, axes["col"]):
            total = total + arrived[block(turn, axes["col"], index)]
        moment = jnp.concatenate([total[4 * tile : 4 * tile + 3, :] for tile in range(tiles)], axis=1)
        weights = jnp.concatenate([total[4 * tile + 3 : 4 * tile + 4, :] for tile in range(tiles)], axis=1)
        third = lax.broadcasted_iota(jnp.int32, moment.shape, 0) == 2
        places, charge = moved_ref[...], charge_of(spec_ref[...])
        force = (charge * (scale * scale)) * ((places - middle) * scale * weights - moment)
        force = force + jnp.where(third, -GRAVITY * charge, 0.0)
        half = ahead_ref[...] + HALF_STEP * force
        ahead_ref[...] = half
        end_ref[...] = force

        @pl.when(turn == 0)
        def move():
            moved_ref[...] = places + TIME_STEP * half / charge
            pack(1)

        return carry

    lax.fori_loop(0, 2, evaluate, 0)


def finish_kernel(moved_ref, ahead_ref, end_ref, trial_ref, momenta_ref, force_ref, sems):
    moves = ((moved_ref, trial_ref), (ahead_ref, momenta_ref), (end_ref, force_ref))
    copies = [pltpu.make_async_copy(source, target, sems.at[which]) for which, (source, target) in enumerate(moves)]
    for copy in copies:
        copy.start()
    for copy in copies:
        copy.wait()


def per_device(row_count, col_count, positions, momenta, species, tile_a, tile_b, tile_count):
    own = positions.shape[1]
    tiles = own // tile_width
    axes = {"col": col_count, "row": row_count}
    vmem = pl.BlockSpec(memory_space=pltpu.VMEM)
    hbm = pl.BlockSpec(memory_space=pltpu.HBM)
    slots = tile_a.shape[-1]
    near_count, far_count = col_count * tiles, row_count * tiles
    own_shape = jax.ShapeDtypeStruct((3, own), f32)
    rows = pltpu.VMEM((2 * near_count * 4, tile_width), f32)
    cols = pltpu.VMEM((2 * far_count * 4, tile_width), f32)
    outs = pl.pallas_call(
        functools.partial(step_kernel, axes, tiles),
        out_shape=(own_shape,) * 3,
        in_specs=[hbm] * 5 + [pl.BlockSpec(memory_space=pltpu.SMEM)],
        out_specs=(vmem,) * 3,
        scratch_shapes=[
            pltpu.VMEM((1, own), jnp.int32), pltpu.VMEM((1, slots), jnp.int32),
            pltpu.SMEM((1, slots), jnp.int32), pltpu.SMEM((1, slots), jnp.int32),
            pltpu.VMEM((2, 4 * tiles, tile_width), f32), rows, cols, rows, rows,
            pltpu.VMEM((near_count, depth, tile_width), f32),
            pltpu.VMEM((near_count, depth, 2 * tile_width), bf16),
            pltpu.VMEM((far_count, depth, tile_width), f32),
            pltpu.VMEM((far_count, tile_width, depth), bf16),
            pltpu.VMEM((far_count, 16, tile_width), f32),
            pltpu.VMEM((far_count, 16, 2 * tile_width), bf16),
            pltpu.VMEM((8 * slots, tile_width), f32),
            pltpu.VMEM((near_count, slots), bf16),
            pltpu.SemaphoreType.DMA((2, 2, col_count + row_count - 2)),
            pltpu.SemaphoreType.DMA((2, 2, col_count - 1)),
            pltpu.SemaphoreType.DMA((6,)),
        ],
        compiler_params=pltpu.CompilerParams(collective_id=0, has_side_effects=True, vmem_limit_bytes=grant),
        name="step",
    )(
        *(
            pltpu.with_memory_space_constraint(array, pltpu.HBM)
            for array in (
                positions, momenta, species.reshape(1, own),
                tile_a.reshape(1, slots), tile_b.reshape(1, slots),
            )
        ),
        tile_count,
    )
    return tuple(
        pl.pallas_call(
            finish_kernel,
            out_shape=(own_shape,) * 3,
            in_specs=[vmem] * 3,
            out_specs=(hbm,) * 3,
            scratch_shapes=[pltpu.SemaphoreType.DMA((3,))],
            compiler_params=pltpu.CompilerParams(vmem_limit_bytes=grant),
            name="finish",
        )(*outs)
    )


def solution(mesh):
    in_specs = (
        P(None, ("row", "col")),
        P(None, ("row", "col")),
        P(("row", "col")),
        P("row", "col", None),
        P("row", "col", None),
        P("row", "col"),
    )
    out_specs = (P(None, ("row", "col")), P(None, ("row", "col")), P(None, ("row", "col")))
    body = functools.partial(per_device, mesh.shape["row"], mesh.shape["col"])
    return jax.shard_map(body, mesh=mesh, in_specs=in_specs, out_specs=out_specs, check_vma=False)
```

```python
import functools
import math

import jax
import jax.numpy as jnp
from jax import lax
from jax.experimental import pallas as pl
from jax.experimental.pallas import tpu as pltpu
from jax.sharding import PartitionSpec as P

SOFTENING = 0.25
GRAVITY = 0.5
LIGHT_CHARGE = 1.0
HEAVY_CHARGE = 2.5
HALF_STEP = 0.1
TIME_STEP = 0.2
tile_width = 128
scale = 1.0 / math.log(2.0)
middle = 2.0
depth = 32
longest = 256
ahead = 8
grant = 48 * 2**20
MESH = pl.DeviceIdType.MESH
f32, bf16 = jnp.float32, jnp.bfloat16


def far_first(axes, name):
    me, size = lax.axis_index(name), axes[name]
    order = []
    for index in range(size - 1):
        down = size - 1 - index
        down = down - jnp.where(down <= me, 1, 0)
        up = index + jnp.where(index >= me, 1, 0)
        order.append({name: jnp.where(2 * me < size, down, up)})
    return order


def remote(source, target, sems, peer):
    return pltpu.make_async_remote_copy(
        src_ref=source,
        dst_ref=target,
        send_sem=sems.at[0],
        recv_sem=sems.at[1],
        device_id=peer,
        device_id_type=MESH,
    )


def await_bytes(region, sem):
    pltpu.make_async_copy(region, region, sem).wait()


def charge_of(species):
    return jnp.where(species == 1, HEAVY_CHARGE, LIGHT_CHARGE).astype(f32)


def pieces(value, number):
    parts = []
    for _ in range(number - 1):
        part = value.astype(bf16).astype(f32)
        parts.append(part)
        value = value - part
    parts.append(value.astype(bf16).astype(f32))
    return parts


pairs_of_pieces = ((0, 0), (0, 1), (1, 0), (0, 2), (2, 0), (1, 1))


def component(ref, start, index, count):
    return ref[pl.ds(start + index, count, stride=4), :]


def table_of(table, tile):
    rows, tiles, lanes = table.shape
    return table.reshape(rows * tiles, lanes)[pl.ds(tile, rows, stride=tiles), :]


def prepare_near(rows, base, near_f, near):
    tiles = near.shape[0]
    for start in range(0, tiles, 8):
        here = pl.ds(start, 8)
        square = 0.0
        for axis in range(3):
            value = (component(rows, base + 4 * start, axis, 8) - middle) * scale
            square = square + value * value
            split = pieces(value, 3)
            for row, (left, _) in enumerate(pairs_of_pieces):
                near_f[6 * axis + row, here, :] = -2.0 * split[left]
        for row, piece in enumerate(pieces(square, 3)):
            near_f[18 + row, here, :] = piece
    for tile in range(tiles):
        single = table_of(near_f, tile).astype(bf16)
        near[tile, :, :tile_width] = single
        near[tile, :, tile_width:] = -single


def prepare_far(cols, base, far_f, far, load_f, load):
    tiles = far.shape[0]
    for start in range(0, tiles, 8):
        here = pl.ds(start, 8)
        charge = component(cols, base + 4 * start, 3, 8)
        square = SOFTENING * scale * scale
        for axis in range(3):
            value = (component(cols, base + 4 * start, axis, 8) - middle) * scale
            square = square + value * value
            split = pieces(value, 3)
            for row, (_, right) in enumerate(pairs_of_pieces):
                far_f[6 * axis + row, here, :] = split[right]
            for row, piece in enumerate(pieces(charge * value, 2)):
                load_f[4 * row + axis, here, :] = piece
        load_f[3, here, :] = charge
        for row, piece in enumerate(pieces(square, 3)):
            far_f[21 + row, here, :] = piece
    for tile in range(tiles):
        far[tile] = table_of(far_f, tile).T.astype(bf16)
        single = table_of(load_f, tile).astype(bf16)
        load[tile, :, :tile_width] = single
        load[tile, :, tile_width:] = single


def visit_pairs(firsts, seconds, near, far, load, terms):
    slots = firsts.shape[1]
    unroll = math.gcd(slots, longest)

    def squares(slot):
        both = jnp.dot(far[seconds[0, slot]], near[firsts[0, slot]], preferred_element_type=f32)
        return both[:, :tile_width], both[:, tile_width:]

    def visit(step, carry):
        start = step * unroll
        ready = [squares(start + index) for index in range(ahead)]
        for index in range(unroll):
            slot = start + index
            square, negative = ready[index]
            if index + ahead < unroll:
                ready.append(squares(slot + ahead))
            inverse = lax.rsqrt(square)
            decay = jnp.exp2(negative * inverse)
            weight = decay * (inverse * inverse) * (inverse + 1.0 / scale)
            high = weight.astype(bf16)
            low = (weight - high.astype(f32)).astype(bf16)
            both = jnp.concatenate([high, low], axis=0)
            term = jnp.dot(load[seconds[0, slot]], both, preferred_element_type=f32)
            terms[pl.ds(pl.multiple_of(8 * slot, 8), 8), :] = term[:8]
        return carry

    lax.fori_loop(0, slots // unroll, visit, 0)


def combine(chosen, terms, partial, base):
    slots = chosen.shape[1]
    tiles = chosen.shape[0]

    def row(index):
        return terms[pl.ds(index, slots, stride=8), :]

    for part in range(4):
        value = row(part) if part == 3 else row(part) + row(4 + part)
        high = value.astype(bf16)
        low = (value - high.astype(f32)).astype(bf16)
        both = jnp.dot(chosen, jnp.concatenate([high, low], axis=1), preferred_element_type=f32)
        partial[pl.ds(base + part, tiles, stride=4), :] = both[:, :tile_width] + both[:, tile_width:]


def step_kernel(
    axes, tiles, pos_hbm, mom_hbm, spec_hbm, first_hbm, second_hbm, count,
    moved_ref, ahead_ref, end_ref,
    spec_ref, first_ref, firsts, seconds,
    packed, rows, cols, partial, arrived,
    near_f, near, far_f, far, load_f, load, terms, chosen,
    sems, fetch_sems,
):
    my_row, my_col = lax.axis_index("row"), lax.axis_index("col")
    across_col, across_row = far_first(axes, "col"), far_first(axes, "row")
    height = 4 * tiles
    barrier = pltpu.get_barrier_semaphore()
    for peer in across_col + across_row:
        pl.semaphore_signal(barrier, inc=1, device_id=peer, device_id_type=MESH)
    moves = (
        (pos_hbm, moved_ref), (spec_hbm, spec_ref), (second_hbm, seconds), (first_hbm, firsts),
        (first_hbm, first_ref), (mom_hbm, ahead_ref),
    )
    fetches = [pltpu.make_async_copy(source, target, fetch_sems.at[which]) for which, (source, target) in enumerate(moves)]
    for fetch in fetches:
        fetch.start()
    for fetch in fetches[:2]:
        fetch.wait()

    def pack(turn):
        places, charge = moved_ref[...], charge_of(spec_ref[...])
        for tile in range(tiles):
            lanes = slice(tile * tile_width, (tile + 1) * tile_width)
            packed[turn, 4 * tile : 4 * tile + 3, :] = places[:, lanes]
            packed[turn, 4 * tile + 3 : 4 * tile + 4, :] = charge[:, lanes]

    def block(turn, size, index):
        return pl.ds(pl.multiple_of((turn * size + index) * height, height), height)

    def prepare_lists():
        near_f[21:24] = jnp.ones((3,) + near_f.shape[1:], f32)
        near_f[24:] = jnp.zeros((depth - 24,) + near_f.shape[1:], f32)
        far_f[18:21] = jnp.ones((3,) + far_f.shape[1:], f32)
        far_f[24:] = jnp.zeros((depth - 24,) + far_f.shape[1:], f32)
        load_f[...] = jnp.zeros_like(load_f)
        for fetch in fetches[2:]:
            fetch.wait()
        tile = lax.broadcasted_iota(jnp.int32, chosen.shape, 0)
        slot = lax.broadcasted_iota(jnp.int32, chosen.shape, 1)
        live = (tile == first_ref[...]) & (slot < count[0, 0])
        chosen[...] = jnp.where(live, 1.0, 0.0).astype(bf16)

    pack(0)
    pl.semaphore_wait(barrier, len(across_col + across_row))

    def evaluate(turn, carry):
        mine, level = block(turn, axes["col"], my_col), block(turn, axes["row"], my_row)
        row_sems, col_sems, sum_sems = (sems.at[turn, which] for which in range(3))
        for peer in across_col:
            remote(packed.at[turn], rows.at[mine], row_sems, peer).start()
        for peer in across_row:
            remote(packed.at[turn], cols.at[level], col_sems, peer).start()
        rows[mine] = packed[turn]
        cols[level] = packed[turn]
        pl.when(turn == 0)(prepare_lists)
        base, col_base = turn * axes["col"] * height, turn * axes["row"] * height
        all_rows = pl.ds(pl.multiple_of(base, height), (axes["col"] - 1) * height)
        all_cols = pl.ds(pl.multiple_of(col_base, height), (axes["row"] - 1) * height)
        await_bytes(cols.at[all_cols], col_sems.at[1])
        prepare_far(cols, col_base, far_f, far, load_f, load)
        await_bytes(rows.at[all_rows], row_sems.at[1])
        prepare_near(rows, base, near_f, near)
        visit_pairs(firsts, seconds, near, far, load, terms)
        combine(chosen[...], terms, partial, base)
        for peer in across_col:
            remote(partial.at[block(turn, axes["col"], peer["col"])], arrived.at[mine], sum_sems, peer).start()
        arrived[mine] = partial[mine]
        await_bytes(arrived.at[all_rows], sum_sems.at[1])
        total = arrived[block(turn, axes["col"], 0)]
        for index in range(1, axes["col"]):
            total = total + arrived[block(turn, axes["col"], index)]
        moment = jnp.concatenate([total[4 * tile : 4 * tile + 3, :] for tile in range(tiles)], axis=1)
        weights = jnp.concatenate([total[4 * tile + 3 : 4 * tile + 4, :] for tile in range(tiles)], axis=1)
        third = lax.broadcasted_iota(jnp.int32, moment.shape, 0) == 2
        places, charge = moved_ref[...], charge_of(spec_ref[...])
        force = (charge * (scale * scale)) * ((places - middle) * scale * weights - moment)
        force = force + jnp.where(third, -GRAVITY * charge, 0.0)
        half = ahead_ref[...] + HALF_STEP * force
        ahead_ref[...] = half
        end_ref[...] = force

        @pl.when(turn == 0)
        def move():
            moved_ref[...] = places + TIME_STEP * half / charge
            pack(1)

        await_bytes(rows.at[all_rows], row_sems.at[0])
        await_bytes(cols.at[all_cols], col_sems.at[0])
        await_bytes(partial.at[all_rows], sum_sems.at[0])
        return carry

    lax.fori_loop(0, 2, evaluate, 0)


def finish_kernel(moved_ref, ahead_ref, end_ref, trial_ref, momenta_ref, force_ref, sems):
    moves = ((moved_ref, trial_ref), (ahead_ref, momenta_ref), (end_ref, force_ref))
    copies = [pltpu.make_async_copy(source, target, sems.at[which]) for which, (source, target) in enumerate(moves)]
    for copy in copies:
        copy.start()
    for copy in copies:
        copy.wait()


def per_device(row_count, col_count, positions, momenta, species, tile_a, tile_b, tile_count):
    own = positions.shape[1]
    tiles = own // tile_width
    axes = {"col": col_count, "row": row_count}
    vmem = pl.BlockSpec(memory_space=pltpu.VMEM)
    hbm = pl.BlockSpec(memory_space=pltpu.HBM)
    slots = tile_a.shape[-1]
    near_count, far_count = col_count * tiles, row_count * tiles
    own_shape = jax.ShapeDtypeStruct((3, own), f32)
    rows = pltpu.VMEM((2 * near_count * 4, tile_width), f32)
    cols = pltpu.VMEM((2 * far_count * 4, tile_width), f32)
    outs = pl.pallas_call(
        functools.partial(step_kernel, axes, tiles),
        out_shape=(own_shape,) * 3,
        in_specs=[hbm] * 5 + [pl.BlockSpec(memory_space=pltpu.SMEM)],
        out_specs=(vmem,) * 3,
        scratch_shapes=[
            pltpu.VMEM((1, own), jnp.int32), pltpu.VMEM((1, slots), jnp.int32),
            pltpu.SMEM((1, slots), jnp.int32), pltpu.SMEM((1, slots), jnp.int32),
            pltpu.VMEM((2, 4 * tiles, tile_width), f32), rows, cols, rows, rows,
            pltpu.VMEM((depth, near_count, tile_width), f32),
            pltpu.VMEM((near_count, depth, 2 * tile_width), bf16),
            pltpu.VMEM((depth, far_count, tile_width), f32),
            pltpu.VMEM((far_count, tile_width, depth), bf16),
            pltpu.VMEM((16, far_count, tile_width), f32),
            pltpu.VMEM((far_count, 16, 2 * tile_width), bf16),
            pltpu.VMEM((8 * slots, tile_width), f32),
            pltpu.VMEM((near_count, slots), bf16),
            pltpu.SemaphoreType.DMA((2, 3, 2)),
            pltpu.SemaphoreType.DMA((6,)),
        ],
        compiler_params=pltpu.CompilerParams(collective_id=0, has_side_effects=True, vmem_limit_bytes=grant),
        name="step",
    )(
        *(
            pltpu.with_memory_space_constraint(array, pltpu.HBM)
            for array in (
                positions, momenta, species.reshape(1, own),
                tile_a.reshape(1, slots), tile_b.reshape(1, slots),
            )
        ),
        tile_count,
    )
    return tuple(
        pl.pallas_call(
            finish_kernel,
            out_shape=(own_shape,) * 3,
            in_specs=[vmem] * 3,
            out_specs=(hbm,) * 3,
            scratch_shapes=[pltpu.SemaphoreType.DMA((3,))],
            compiler_params=pltpu.CompilerParams(vmem_limit_bytes=grant),
            name="finish",
        )(*outs)
    )


def solution(mesh):
    in_specs = (
        P(None, ("row", "col")),
        P(None, ("row", "col")),
        P(("row", "col")),
        P("row", "col", None),
        P("row", "col", None),
        P("row", "col"),
    )
    out_specs = (P(None, ("row", "col")), P(None, ("row", "col")), P(None, ("row", "col")))
    body = functools.partial(per_device, mesh.shape["row"], mesh.shape["col"])
    return jax.shard_map(body, mesh=mesh, in_specs=in_specs, out_specs=out_specs, check_vma=False)
```

```python
import functools
import math

import jax
import jax.numpy as jnp
from jax import lax
from jax.experimental import pallas as pl
from jax.experimental.pallas import tpu as pltpu
from jax.sharding import PartitionSpec as P

SOFTENING = 0.25
GRAVITY = 0.5
LIGHT_CHARGE = 1.0
HEAVY_CHARGE = 2.5
HALF_STEP = 0.1
TIME_STEP = 0.2
tile_width = 128
scale = 1.0 / math.log(2.0)
middle = 2.0
depth = 32
longest = 256
ahead = 8
grant = 48 * 2**20
MESH = pl.DeviceIdType.MESH
f32, bf16 = jnp.float32, jnp.bfloat16


def far_first(axes, name):
    me, size = lax.axis_index(name), axes[name]
    order = []
    for index in range(size - 1):
        down = size - 1 - index
        down = down - jnp.where(down <= me, 1, 0)
        up = index + jnp.where(index >= me, 1, 0)
        order.append({name: jnp.where(2 * me < size, down, up)})
    return order


def remote(source, target, sems, peer):
    return pltpu.make_async_remote_copy(
        src_ref=source,
        dst_ref=target,
        send_sem=sems.at[0],
        recv_sem=sems.at[1],
        device_id=peer,
        device_id_type=MESH,
    )


def await_bytes(region, sem):
    pltpu.make_async_copy(region, region, sem).wait()


def charge_of(species):
    return jnp.where(species == 1, HEAVY_CHARGE, LIGHT_CHARGE).astype(f32)


def pieces(value, number):
    parts = []
    for _ in range(number - 1):
        part = value.astype(bf16).astype(f32)
        parts.append(part)
        value = value - part
    parts.append(value.astype(bf16).astype(f32))
    return parts


pairs_of_pieces = ((0, 0), (0, 1), (1, 0), (0, 2), (2, 0), (1, 1))


def component(ref, start, index, count):
    return ref[pl.ds(start + index, count, stride=4), :]


def table_of(table, tile):
    rows, tiles, lanes = table.shape
    return table.reshape(rows * tiles, lanes)[pl.ds(tile, rows, stride=tiles), :]


def prepare_near(rows, base, near_f, near):
    tiles = near.shape[0]
    for start in range(0, tiles, 8):
        here = pl.ds(start, 8)
        square = 0.0
        for axis in range(3):
            value = (component(rows, base + 4 * start, axis, 8) - middle) * scale
            square = square + value * value
            split = pieces(value, 3)
            for row, (left, _) in enumerate(pairs_of_pieces):
                near_f[6 * axis + row, here, :] = -2.0 * split[left]
        for row, piece in enumerate(pieces(square, 3)):
            near_f[18 + row, here, :] = piece
    for tile in range(tiles):
        single = table_of(near_f, tile).astype(bf16)
        near[tile, :, :tile_width] = single
        near[tile, :, tile_width:] = -single


def prepare_far(cols, base, far_f, far, load_f, load):
    tiles = far.shape[0]
    for start in range(0, tiles, 8):
        here = pl.ds(start, 8)
        charge = component(cols, base + 4 * start, 3, 8)
        square = SOFTENING * scale * scale
        for axis in range(3):
            value = (component(cols, base + 4 * start, axis, 8) - middle) * scale
            square = square + value * value
            split = pieces(value, 3)
            for row, (_, right) in enumerate(pairs_of_pieces):
                far_f[6 * axis + row, here, :] = split[right]
            for row, piece in enumerate(pieces(charge * value, 2)):
                load_f[4 * row + axis, here, :] = piece
        load_f[3, here, :] = charge
        for row, piece in enumerate(pieces(square, 3)):
            far_f[21 + row, here, :] = piece
    for tile in range(tiles):
        far[tile] = table_of(far_f, tile).T.astype(bf16)
        single = table_of(load_f, tile).astype(bf16)
        load[tile, :, :tile_width] = single
        load[tile, :, tile_width:] = single


def visit_pairs(firsts, seconds, near, far, load, terms):
    slots = firsts.shape[1]
    unroll = math.gcd(slots, longest)

    def squares(slot):
        both = jnp.dot(far[seconds[0, slot]], near[firsts[0, slot]], preferred_element_type=f32)
        return both[:, :tile_width], both[:, tile_width:]

    def visit(step, carry):
        start = step * unroll
        ready = [squares(start + index) for index in range(ahead)]
        for index in range(unroll):
            slot = start + index
            square, negative = ready[index]
            if index + ahead < unroll:
                ready.append(squares(slot + ahead))
            inverse = lax.rsqrt(square)
            decay = jnp.exp2(negative * inverse)
            weight = decay * (inverse * inverse) * (inverse + 1.0 / scale)
            high = weight.astype(bf16)
            low = (weight - high.astype(f32)).astype(bf16)
            both = jnp.concatenate([high, low], axis=0)
            term = jnp.dot(load[seconds[0, slot]], both, preferred_element_type=f32)
            terms[pl.ds(pl.multiple_of(8 * slot, 8), 8), :] = term[:8]
        return carry

    if slots == unroll:
        visit(0, 0)
    else:
        lax.fori_loop(0, slots // unroll, visit, 0)


def combine(chosen, terms, partial, base):
    slots = chosen.shape[1]
    tiles = chosen.shape[0]

    def row(index):
        return terms[pl.ds(index, slots, stride=8), :]

    for part in range(4):
        value = row(part) if part == 3 else row(part) + row(4 + part)
        high = value.astype(bf16)
        low = (value - high.astype(f32)).astype(bf16)
        both = jnp.dot(chosen, jnp.concatenate([high, low], axis=1), preferred_element_type=f32)
        partial[pl.ds(base + part, tiles, stride=4), :] = both[:, :tile_width] + both[:, tile_width:]


def tiled(target, places, last, tiles):
    for tile in range(tiles):
        lanes = slice(tile * tile_width, (tile + 1) * tile_width)
        target[4 * tile : 4 * tile + 3, :] = places[:, lanes]
        target[4 * tile + 3 : 4 * tile + 4, :] = last[:, lanes]


def untiled(block, first, count, tiles):
    return jnp.concatenate([block[4 * tile + first : 4 * tile + first + count, :] for tile in range(tiles)], axis=1)


def force_of(total, places, charge, tiles):
    moment, weights = untiled(total, 0, 3, tiles), untiled(total, 3, 1, tiles)
    third = lax.broadcasted_iota(jnp.int32, moment.shape, 0) == 2
    force = (charge * (scale * scale)) * ((places - middle) * scale * weights - moment)
    return force + jnp.where(third, -GRAVITY * charge, 0.0)


def step_kernel(
    axes, tiles, pos_hbm, mom_hbm, spec_hbm, first_hbm, second_hbm, count,
    moved_ref, ahead_ref, end_ref,
    spec_ref, first_ref, firsts, seconds,
    packed, twin_packed, twin_momenta, kicked, rows, cols, partial, arrived,
    near_f, near, far_f, far, load_f, load, terms, chosen,
    sems, fetch_sems,
):
    my_row, my_col = lax.axis_index("row"), lax.axis_index("col")
    col_count, row_count = axes["col"], axes["row"]
    across_col, across_row = far_first(axes, "col"), far_first(axes, "row")
    odd = lax.rem(my_row, 2)
    twin = my_row + 1 - 2 * odd
    across_twin = [{"row": twin, "col": peer["col"]} for peer in across_col] + [{"row": twin, "col": my_col}]
    height = 4 * tiles
    row_a, col_a, momenta_sems, sum_own, sum_twin, row_b, col_b, kick_sems, sum_b = (sems.at[which] for which in range(9))
    barrier = pltpu.get_barrier_semaphore()
    everyone = across_col + across_row + across_twin[:-1]
    for peer in everyone:
        pl.semaphore_signal(barrier, inc=1, device_id=peer, device_id_type=MESH)
    moves = (
        (pos_hbm, moved_ref), (spec_hbm, spec_ref), (mom_hbm, ahead_ref), (second_hbm, seconds), (first_hbm, firsts),
        (first_hbm, first_ref),
    )
    fetches = [pltpu.make_async_copy(source, target, fetch_sems.at[which]) for which, (source, target) in enumerate(moves)]
    for fetch in fetches:
        fetch.start()
    for fetch in fetches[:2]:
        fetch.wait()

    def block(size, turn, index):
        return pl.ds(pl.multiple_of((turn * size + index) * height, height), height)

    def several(count):
        return pl.ds(0, count * height)

    def send_packed(source, turn, row_targets, level, row_sems, col_sems):
        for peer in row_targets:
            remote(source, rows.at[block(col_count, turn, my_col)], row_sems, peer).start()
        for peer in across_row:
            remote(source, cols.at[block(row_count, turn, level)], col_sems, peer).start()

    def first_gather():
        send_packed(packed.at[0], 0, across_col, my_row, row_a, col_a)
        rows[block(col_count, 0, my_col)] = packed[0]
        cols[block(row_count, 0, my_row)] = packed[0]
        near_f[21:24] = jnp.ones((3,) + near_f.shape[1:], f32)
        near_f[24:] = jnp.zeros((depth - 24,) + near_f.shape[1:], f32)
        far_f[18:21] = jnp.ones((3,) + far_f.shape[1:], f32)
        far_f[24:] = jnp.zeros((depth - 24,) + far_f.shape[1:], f32)
        load_f[...] = jnp.zeros_like(load_f)
        for fetch in fetches[2:]:
            fetch.wait()

        @pl.when(odd == 0)
        def lend_momenta():
            tiled(kicked, ahead_ref[...], jnp.zeros((1, ahead_ref.shape[1]), f32), tiles)
            remote(kicked, twin_momenta, momenta_sems, across_twin[-1]).start()

        tile = lax.broadcasted_iota(jnp.int32, chosen.shape, 0)
        slot = lax.broadcasted_iota(jnp.int32, chosen.shape, 1)
        live = (tile == first_ref[...]) & (slot < count[0, 0])
        chosen[...] = jnp.where(live, 1.0, 0.0).astype(bf16)

    tiled(packed.at[0], moved_ref[...], charge_of(spec_ref[...]), tiles)
    pl.semaphore_wait(barrier, len(everyone))

    def on(turn, wanted, parity=None):
        return turn == wanted if parity is None else (turn == wanted) & (odd == parity)

    def kick(total, places, momenta, charge):
        half = momenta + HALF_STEP * force_of(total, places, charge, tiles)
        return half, places + TIME_STEP * half / charge

    def added(start):
        total = arrived[block(col_count, start, 0)]
        for index in range(1, col_count):
            total = total + arrived[block(col_count, start, index)]
        return total

    def evaluate(turn, carry):
        pl.when(on(turn, 0))(first_gather)
        for wanted, parity, number in ((0, None, row_count - 1), (1, 0, row_count), (1, 1, row_count - 2)):
            @pl.when(on(turn, wanted, parity))
            def columns_arrive():
                await_bytes(cols.at[several(number)], (col_b if wanted else col_a).at[1])
        base, col_base = turn * col_count * height, turn * row_count * height
        prepare_far(cols, col_base, far_f, far, load_f, load)
        for wanted, parity, number in ((0, None, col_count - 1), (1, 0, col_count), (1, 1, col_count - 1)):
            @pl.when(on(turn, wanted, parity))
            def rows_arrive():
                await_bytes(rows.at[several(number)], (row_b if wanted else row_a).at[1])
        prepare_near(rows, base, near_f, near)
        visit_pairs(firsts, seconds, near, far, load, terms)
        combine(chosen[...], terms, partial, base)

        def send_partial(peer, target, pair):
            source = partial.at[block(col_count, turn, peer["col"])]
            remote(source, arrived.at[block(col_count, target, my_col)], pair, peer).start()

        @pl.when(on(turn, 0, 0))
        def lend_sums():
            for peer in across_twin:
                send_partial(peer, 1, sum_twin)
            await_bytes(kicked, momenta_sems.at[0])
            await_bytes(partial.at[several(col_count)], sum_twin.at[0])

        @pl.when(on(turn, 0, 1))
        def move():
            for peer in across_col:
                send_partial(peer, 0, sum_own)
            arrived[block(col_count, 0, my_col)] = partial[block(col_count, turn, my_col)]
            await_bytes(twin_momenta, momenta_sems.at[1])
            await_bytes(arrived.at[several(col_count)], sum_twin.at[1])
            other = cols[block(row_count, 0, twin)]
            charge = untiled(other, 3, 1, tiles)
            momenta = untiled(twin_momenta[...], 0, 3, tiles)
            half, moved = kick(added(1), untiled(other, 0, 3, tiles), momenta, charge)
            tiled(twin_packed, moved, charge, tiles)
            send_packed(twin_packed, 1, across_twin, twin, row_b, col_b)
            cols[block(row_count, 1, twin)] = twin_packed[...]
            await_bytes(arrived.at[several(col_count - 1)], sum_own.at[1])
            tiled(kicked, half, charge, tiles)
            charge = charge_of(spec_ref[...])
            half, moved = kick(added(0), moved_ref[...], ahead_ref[...], charge)
            ahead_ref[...] = half
            moved_ref[...] = moved
            tiled(packed.at[1], moved, charge, tiles)
            send_packed(packed.at[1], 1, across_col, my_row, row_b, col_b)
            remote(kicked, twin_momenta, kick_sems, across_twin[-1]).start()
            rows[block(col_count, 1, my_col)] = packed[1]
            cols[block(row_count, 1, my_row)] = packed[1]
            await_bytes(partial.at[several(col_count - 1)], sum_own.at[0])

        @pl.when(on(turn, 1))
        def end():
            for peer in across_col:
                send_partial(peer, 2, sum_b)
            arrived[block(col_count, 2, my_col)] = partial[block(col_count, turn, my_col)]

            @pl.when(odd == 0)
            def take_back():
                await_bytes(twin_momenta, kick_sems.at[1])
                moved_ref[...] = untiled(rows[block(col_count, 1, my_col)], 0, 3, tiles)
                ahead_ref[...] = untiled(twin_momenta[...], 0, 3, tiles)

            @pl.when(odd == 1)
            def sent():
                await_bytes(kicked, kick_sems.at[0])
                await_bytes(rows.at[several(2 * col_count - 1)], row_b.at[0])
                await_bytes(cols.at[several(2 * row_count - 2)], col_b.at[0])

            await_bytes(arrived.at[several(col_count - 1)], sum_b.at[1])
            force = force_of(added(2), moved_ref[...], charge_of(spec_ref[...]), tiles)
            ahead_ref[...] = ahead_ref[...] + HALF_STEP * force
            end_ref[...] = force
            await_bytes(rows.at[several(col_count - 1)], row_a.at[0])
            await_bytes(cols.at[several(row_count - 1)], col_a.at[0])
            await_bytes(partial.at[several(col_count - 1)], sum_b.at[0])

        return carry

    lax.fori_loop(0, 2, evaluate, 0)


def finish_kernel(moved_ref, ahead_ref, end_ref, trial_ref, momenta_ref, force_ref, sems):
    moves = ((moved_ref, trial_ref), (ahead_ref, momenta_ref), (end_ref, force_ref))
    copies = [pltpu.make_async_copy(source, target, sems.at[which]) for which, (source, target) in enumerate(moves)]
    for copy in copies:
        copy.start()
    for copy in copies:
        copy.wait()


def per_device(row_count, col_count, positions, momenta, species, tile_a, tile_b, tile_count):
    own = positions.shape[1]
    tiles = own // tile_width
    axes = {"col": col_count, "row": row_count}
    vmem = pl.BlockSpec(memory_space=pltpu.VMEM)
    hbm = pl.BlockSpec(memory_space=pltpu.HBM)
    slots = tile_a.shape[-1]
    near_count, far_count = col_count * tiles, row_count * tiles
    own_shape = jax.ShapeDtypeStruct((3, own), f32)
    tiled_block = pltpu.VMEM((4 * tiles, tile_width), f32)
    rows = pltpu.VMEM((2 * near_count * 4, tile_width), f32)
    cols = pltpu.VMEM((2 * far_count * 4, tile_width), f32)
    outs = pl.pallas_call(
        functools.partial(step_kernel, axes, tiles),
        out_shape=(own_shape,) * 3,
        in_specs=[hbm] * 5 + [pl.BlockSpec(memory_space=pltpu.SMEM)],
        out_specs=(vmem,) * 3,
        scratch_shapes=[
            pltpu.VMEM((1, own), jnp.int32), pltpu.VMEM((1, slots), jnp.int32),
            pltpu.SMEM((1, slots), jnp.int32), pltpu.SMEM((1, slots), jnp.int32),
            pltpu.VMEM((2, 4 * tiles, tile_width), f32), tiled_block, tiled_block, tiled_block,
            rows, cols, rows, pltpu.VMEM((3 * near_count * 4, tile_width), f32),
            pltpu.VMEM((depth, near_count, tile_width), f32),
            pltpu.VMEM((near_count, depth, 2 * tile_width), bf16),
            pltpu.VMEM((depth, far_count, tile_width), f32),
            pltpu.VMEM((far_count, tile_width, depth), bf16),
            pltpu.VMEM((16, far_count, tile_width), f32),
            pltpu.VMEM((far_count, 16, 2 * tile_width), bf16),
            pltpu.VMEM((8 * slots, tile_width), f32),
            pltpu.VMEM((near_count, slots), bf16),
            pltpu.SemaphoreType.DMA((9, 2)),
            pltpu.SemaphoreType.DMA((6,)),
        ],
        compiler_params=pltpu.CompilerParams(collective_id=0, has_side_effects=True, vmem_limit_bytes=grant),
        name="step",
    )(
        *(
            pltpu.with_memory_space_constraint(array, pltpu.HBM)
            for array in (
                positions, momenta, species.reshape(1, own),
                tile_a.reshape(1, slots), tile_b.reshape(1, slots),
            )
        ),
        tile_count,
    )
    return tuple(
        pl.pallas_call(
            finish_kernel,
            out_shape=(own_shape,) * 3,
            in_specs=[vmem] * 3,
            out_specs=(hbm,) * 3,
            scratch_shapes=[pltpu.SemaphoreType.DMA((3,))],
            compiler_params=pltpu.CompilerParams(vmem_limit_bytes=grant),
            name="finish",
        )(*outs)
    )


def solution(mesh):
    in_specs = (
        P(None, ("row", "col")),
        P(None, ("row", "col")),
        P(("row", "col")),
        P("row", "col", None),
        P("row", "col", None),
        P("row", "col"),
    )
    out_specs = (P(None, ("row", "col")), P(None, ("row", "col")), P(None, ("row", "col")))
    body = functools.partial(per_device, mesh.shape["row"], mesh.shape["col"])
    return jax.shard_map(body, mesh=mesh, in_specs=in_specs, out_specs=out_specs, check_vma=False)
```

```python
import functools
import math

import jax
import jax.numpy as jnp
from jax import lax
from jax.experimental import pallas as pl
from jax.experimental.pallas import tpu as pltpu
from jax.sharding import PartitionSpec as P

SOFTENING = 0.25
GRAVITY = 0.5
LIGHT_CHARGE = 1.0
HEAVY_CHARGE = 2.5
HALF_STEP = 0.1
TIME_STEP = 0.2
tile_width = 128
scale = 1.0 / math.log(2.0)
middle = 2.0
depth = 32
longest = 256
ahead = 8
grant = 48 * 2**20
MESH = pl.DeviceIdType.MESH
f32, bf16 = jnp.float32, jnp.bfloat16


def far_first(axes, name):
    me, size = lax.axis_index(name), axes[name]
    order = []
    for index in range(size - 1):
        down = size - 1 - index
        down = down - jnp.where(down <= me, 1, 0)
        up = index + jnp.where(index >= me, 1, 0)
        order.append({name: jnp.where(2 * me < size, down, up)})
    return order


def remote(source, target, sems, peer):
    return pltpu.make_async_remote_copy(
        src_ref=source,
        dst_ref=target,
        send_sem=sems.at[0],
        recv_sem=sems.at[1],
        device_id=peer,
        device_id_type=MESH,
    )


def await_bytes(region, sem):
    pltpu.make_async_copy(region, region, sem).wait()


def charge_of(species):
    return jnp.where(species == 1, HEAVY_CHARGE, LIGHT_CHARGE).astype(f32)


def pieces(value, number):
    parts = []
    for _ in range(number - 1):
        part = value.astype(bf16).astype(f32)
        parts.append(part)
        value = value - part
    parts.append(value.astype(bf16).astype(f32))
    return parts


pairs_of_pieces = ((0, 0), (0, 1), (1, 0), (0, 2), (2, 0), (1, 1))


def component(ref, start, index, count):
    return ref[pl.ds(start + index, count, stride=4), :]


def table_of(table, tile):
    rows, tiles, lanes = table.shape
    return table.reshape(rows * tiles, lanes)[pl.ds(tile, rows, stride=tiles), :]


def prepare_near(rows, base, near_f, near):
    tiles = near.shape[0]
    for start in range(0, tiles, 8):
        here = pl.ds(start, 8)
        square = 0.0
        for axis in range(3):
            value = (component(rows, base + 4 * start, axis, 8) - middle) * scale
            square = square + value * value
            split = pieces(value, 3)
            for row, (left, _) in enumerate(pairs_of_pieces):
                near_f[6 * axis + row, here, :] = -2.0 * split[left]
        for row, piece in enumerate(pieces(square, 3)):
            near_f[18 + row, here, :] = piece
    for tile in range(tiles):
        single = table_of(near_f, tile).astype(bf16)
        near[tile, :, :tile_width] = single
        near[tile, :, tile_width:] = -single


def prepare_far(cols, base, far_f, far, load_f, load):
    tiles = far.shape[0]
    for start in range(0, tiles, 8):
        here = pl.ds(start, 8)
        charge = component(cols, base + 4 * start, 3, 8)
        square = SOFTENING * scale * scale
        for axis in range(3):
            value = (component(cols, base + 4 * start, axis, 8) - middle) * scale
            square = square + value * value
            split = pieces(value, 3)
            for row, (_, right) in enumerate(pairs_of_pieces):
                far_f[6 * axis + row, here, :] = split[right]
            for row, piece in enumerate(pieces(charge * value, 2)):
                load_f[4 * row + axis, here, :] = piece
        load_f[3, here, :] = charge
        for row, piece in enumerate(pieces(square, 3)):
            far_f[21 + row, here, :] = piece
    for tile in range(tiles):
        far[tile] = table_of(far_f, tile).T.astype(bf16)
        single = table_of(load_f, tile).astype(bf16)
        load[tile, :, :tile_width] = single
        load[tile, :, tile_width:] = single


def visit_pairs(firsts, seconds, near, far, load, terms):
    slots = firsts.shape[1]
    unroll = math.gcd(slots, longest)

    def squares(slot):
        both = jnp.dot(far[seconds[0, slot]], near[firsts[0, slot]], preferred_element_type=f32)
        return both[:, :tile_width], both[:, tile_width:]

    def visit(step, carry):
        start = step * unroll
        ready = [squares(start + index) for index in range(ahead)]
        for index in range(unroll):
            slot = start + index
            square, negative = ready[index]
            if index + ahead < unroll:
                ready.append(squares(slot + ahead))
            inverse = lax.rsqrt(square)
            decay = jnp.exp2(negative * inverse)
            weight = decay * (inverse * inverse) * (inverse + 1.0 / scale)
            high = weight.astype(bf16)
            low = (weight - high.astype(f32)).astype(bf16)
            both = jnp.concatenate([high, low], axis=0)
            term = jnp.dot(load[seconds[0, slot]], both, preferred_element_type=f32)
            terms[pl.ds(pl.multiple_of(8 * slot, 8), 8), :] = term[:8]
        return carry

    if slots == unroll:
        visit(0, 0)
    else:
        lax.fori_loop(0, slots // unroll, visit, 0)


def combine(chosen, terms, partial, base):
    slots = chosen.shape[1]
    tiles = chosen.shape[0]

    def row(index):
        return terms[pl.ds(index, slots, stride=8), :]

    for part in range(4):
        value = row(part) if part == 3 else row(part) + row(4 + part)
        high = value.astype(bf16)
        low = (value - high.astype(f32)).astype(bf16)
        both = jnp.dot(chosen, jnp.concatenate([high, low], axis=1), preferred_element_type=f32)
        partial[pl.ds(base + part, tiles, stride=4), :] = both[:, :tile_width] + both[:, tile_width:]


def tiled(target, places, last, tiles):
    for tile in range(tiles):
        lanes = slice(tile * tile_width, (tile + 1) * tile_width)
        target[4 * tile : 4 * tile + 3, :] = places[:, lanes]
        target[4 * tile + 3 : 4 * tile + 4, :] = last[:, lanes]


def untiled(block, first, count, tiles):
    return jnp.concatenate([block[4 * tile + first : 4 * tile + first + count, :] for tile in range(tiles)], axis=1)


def terms_of(places, charge):
    third = lax.broadcasted_iota(jnp.int32, places.shape, 0) == 2
    return charge * (scale * scale), (places - middle) * scale, jnp.where(third, -GRAVITY * charge, 0.0)


def force_of(total, known, tiles):
    factor, places, weight = known
    return factor * (places * untiled(total, 3, 1, tiles) - untiled(total, 0, 3, tiles)) + weight


def step_kernel(
    axes, tiles, pos_hbm, mom_hbm, spec_hbm, first_hbm, second_hbm, count,
    moved_ref, ahead_ref, end_ref,
    spec_ref, first_ref, firsts, seconds,
    packed, twin_packed, twin_momenta, kicked, rows, cols, partial, arrived,
    near_f, near, far_f, far, load_f, load, terms, chosen,
    sems, fetch_sems,
):
    my_row, my_col = lax.axis_index("row"), lax.axis_index("col")
    col_count, row_count = axes["col"], axes["row"]
    across_col, across_row = far_first(axes, "col"), far_first(axes, "row")
    odd = lax.rem(my_row, 2)
    twin = my_row + 1 - 2 * odd
    across_twin = [{"row": twin, "col": peer["col"]} for peer in across_col] + [{"row": twin, "col": my_col}]
    height = 4 * tiles
    row_a, col_a, momenta_sems, sum_own, sum_twin, row_b, col_b, kick_sems, sum_b = (sems.at[which] for which in range(9))
    barrier = pltpu.get_barrier_semaphore()
    everyone = across_col + across_row + across_twin[:-1]
    for peer in everyone:
        pl.semaphore_signal(barrier, inc=1, device_id=peer, device_id_type=MESH)
    moves = (
        (pos_hbm, moved_ref), (spec_hbm, spec_ref), (mom_hbm, ahead_ref), (second_hbm, seconds), (first_hbm, firsts),
        (first_hbm, first_ref),
    )
    fetches = [pltpu.make_async_copy(source, target, fetch_sems.at[which]) for which, (source, target) in enumerate(moves)]
    for fetch in fetches:
        fetch.start()
    for fetch in fetches[:2]:
        fetch.wait()

    def block(size, turn, index):
        return pl.ds(pl.multiple_of((turn * size + index) * height, height), height)

    def several(count):
        return pl.ds(0, count * height)

    def send_packed(source, turn, row_targets, level, row_sems, col_sems):
        for peer in row_targets:
            remote(source, rows.at[block(col_count, turn, my_col)], row_sems, peer).start()
        for peer in across_row:
            remote(source, cols.at[block(row_count, turn, level)], col_sems, peer).start()

    def first_gather():
        send_packed(packed.at[0], 0, across_col, my_row, row_a, col_a)
        rows[block(col_count, 0, my_col)] = packed[0]
        cols[block(row_count, 0, my_row)] = packed[0]
        near_f[21:24] = jnp.ones((3,) + near_f.shape[1:], f32)
        near_f[24:] = jnp.zeros((depth - 24,) + near_f.shape[1:], f32)
        far_f[18:21] = jnp.ones((3,) + far_f.shape[1:], f32)
        far_f[24:] = jnp.zeros((depth - 24,) + far_f.shape[1:], f32)
        load_f[...] = jnp.zeros_like(load_f)
        for fetch in fetches[2:]:
            fetch.wait()

        @pl.when(odd == 0)
        def lend_momenta():
            tiled(kicked, ahead_ref[...], jnp.zeros((1, ahead_ref.shape[1]), f32), tiles)
            remote(kicked, twin_momenta, momenta_sems, across_twin[-1]).start()

        tile = lax.broadcasted_iota(jnp.int32, chosen.shape, 0)
        slot = lax.broadcasted_iota(jnp.int32, chosen.shape, 1)
        live = (tile == first_ref[...]) & (slot < count[0, 0])
        chosen[...] = jnp.where(live, 1.0, 0.0).astype(bf16)

    tiled(packed.at[0], moved_ref[...], charge_of(spec_ref[...]), tiles)
    pl.semaphore_wait(barrier, len(everyone))

    def on(turn, wanted, parity=None):
        return turn == wanted if parity is None else (turn == wanted) & (odd == parity)

    def kick(start, known, places, momenta, rate):
        half = momenta + HALF_STEP * force_of(added(start), known, tiles)
        return half, places + rate * half

    def added(start):
        total = arrived[block(col_count, start, 0)]
        for index in range(1, col_count):
            total = total + arrived[block(col_count, start, index)]
        return total

    def evaluate(turn, carry):
        pl.when(on(turn, 0))(first_gather)
        for wanted, parity, number in ((0, None, row_count - 1), (1, 0, row_count), (1, 1, row_count - 2)):
            @pl.when(on(turn, wanted, parity))
            def columns_arrive():
                await_bytes(cols.at[several(number)], (col_b if wanted else col_a).at[1])
        base, col_base = turn * col_count * height, turn * row_count * height
        prepare_far(cols, col_base, far_f, far, load_f, load)
        for wanted, parity, number in ((0, None, col_count - 1), (1, 0, col_count), (1, 1, col_count - 1)):
            @pl.when(on(turn, wanted, parity))
            def rows_arrive():
                await_bytes(rows.at[several(number)], (row_b if wanted else row_a).at[1])
        prepare_near(rows, base, near_f, near)
        visit_pairs(firsts, seconds, near, far, load, terms)
        combine(chosen[...], terms, partial, base)

        def send_partial(peer, target, pair):
            source = partial.at[block(col_count, turn, peer["col"])]
            remote(source, arrived.at[block(col_count, target, my_col)], pair, peer).start()

        @pl.when(on(turn, 0, 0))
        def lend_sums():
            for peer in across_twin:
                send_partial(peer, 1, sum_twin)
            await_bytes(kicked, momenta_sems.at[0])
            await_bytes(partial.at[several(col_count)], sum_twin.at[0])

        @pl.when(on(turn, 0, 1))
        def move():
            for peer in across_col:
                send_partial(peer, 0, sum_own)
            arrived[block(col_count, 0, my_col)] = partial[block(col_count, turn, my_col)]
            charge, places, momenta = charge_of(spec_ref[...]), moved_ref[...], ahead_ref[...]
            known, rate = terms_of(places, charge), TIME_STEP / charge
            await_bytes(arrived.at[several(col_count - 1)], sum_own.at[1])
            half, moved = kick(0, known, places, momenta, rate)
            tiled(packed.at[1], moved, charge, tiles)
            send_packed(packed.at[1], 1, across_col, my_row, row_b, col_b)
            ahead_ref[...] = half
            moved_ref[...] = moved
            await_bytes(twin_momenta, momenta_sems.at[1])
            other = cols[block(row_count, 0, twin)]
            charge, places = untiled(other, 3, 1, tiles), untiled(other, 0, 3, tiles)
            momenta = untiled(twin_momenta[...], 0, 3, tiles)
            known, rate = terms_of(places, charge), TIME_STEP / charge
            await_bytes(arrived.at[several(col_count)], sum_twin.at[1])
            half, moved = kick(1, known, places, momenta, rate)
            tiled(twin_packed, moved, charge, tiles)
            send_packed(twin_packed, 1, across_twin, twin, row_b, col_b)
            cols[block(row_count, 1, twin)] = twin_packed[...]
            tiled(kicked, half, charge, tiles)
            remote(kicked, twin_momenta, kick_sems, across_twin[-1]).start()
            rows[block(col_count, 1, my_col)] = packed[1]
            cols[block(row_count, 1, my_row)] = packed[1]
            await_bytes(partial.at[several(col_count - 1)], sum_own.at[0])

        @pl.when(on(turn, 1))
        def end():
            for peer in across_col:
                send_partial(peer, 2, sum_b)
            arrived[block(col_count, 2, my_col)] = partial[block(col_count, turn, my_col)]

            @pl.when(odd == 0)
            def take_back():
                await_bytes(twin_momenta, kick_sems.at[1])
                moved_ref[...] = untiled(rows[block(col_count, 1, my_col)], 0, 3, tiles)
                ahead_ref[...] = untiled(twin_momenta[...], 0, 3, tiles)

            @pl.when(odd == 1)
            def sent():
                await_bytes(kicked, kick_sems.at[0])
                await_bytes(rows.at[several(2 * col_count - 1)], row_b.at[0])
                await_bytes(cols.at[several(2 * row_count - 2)], col_b.at[0])

            known, momenta = terms_of(moved_ref[...], charge_of(spec_ref[...])), ahead_ref[...]
            await_bytes(arrived.at[several(col_count - 1)], sum_b.at[1])
            force = force_of(added(2), known, tiles)
            ahead_ref[...] = momenta + HALF_STEP * force
            end_ref[...] = force
            await_bytes(rows.at[several(col_count - 1)], row_a.at[0])
            await_bytes(cols.at[several(row_count - 1)], col_a.at[0])
            await_bytes(partial.at[several(col_count - 1)], sum_b.at[0])

        return carry

    lax.fori_loop(0, 2, evaluate, 0)


def finish_kernel(moved_ref, ahead_ref, end_ref, trial_ref, momenta_ref, force_ref, sems):
    moves = ((moved_ref, trial_ref), (ahead_ref, momenta_ref), (end_ref, force_ref))
    copies = [pltpu.make_async_copy(source, target, sems.at[which]) for which, (source, target) in enumerate(moves)]
    for copy in copies:
        copy.start()
    for copy in copies:
        copy.wait()


def per_device(row_count, col_count, positions, momenta, species, tile_a, tile_b, tile_count):
    own = positions.shape[1]
    tiles = own // tile_width
    axes = {"col": col_count, "row": row_count}
    vmem = pl.BlockSpec(memory_space=pltpu.VMEM)
    hbm = pl.BlockSpec(memory_space=pltpu.HBM)
    slots = tile_a.shape[-1]
    near_count, far_count = col_count * tiles, row_count * tiles
    own_shape = jax.ShapeDtypeStruct((3, own), f32)
    tiled_block = pltpu.VMEM((4 * tiles, tile_width), f32)
    rows = pltpu.VMEM((2 * near_count * 4, tile_width), f32)
    cols = pltpu.VMEM((2 * far_count * 4, tile_width), f32)
    outs = pl.pallas_call(
        functools.partial(step_kernel, axes, tiles),
        out_shape=(own_shape,) * 3,
        in_specs=[hbm] * 5 + [pl.BlockSpec(memory_space=pltpu.SMEM)],
        out_specs=(vmem,) * 3,
        scratch_shapes=[
            pltpu.VMEM((1, own), jnp.int32), pltpu.VMEM((1, slots), jnp.int32),
            pltpu.SMEM((1, slots), jnp.int32), pltpu.SMEM((1, slots), jnp.int32),
            pltpu.VMEM((2, 4 * tiles, tile_width), f32), tiled_block, tiled_block, tiled_block,
            rows, cols, rows, pltpu.VMEM((3 * near_count * 4, tile_width), f32),
            pltpu.VMEM((depth, near_count, tile_width), f32),
            pltpu.VMEM((near_count, depth, 2 * tile_width), bf16),
            pltpu.VMEM((depth, far_count, tile_width), f32),
            pltpu.VMEM((far_count, tile_width, depth), bf16),
            pltpu.VMEM((16, far_count, tile_width), f32),
            pltpu.VMEM((far_count, 16, 2 * tile_width), bf16),
            pltpu.VMEM((8 * slots, tile_width), f32),
            pltpu.VMEM((near_count, slots), bf16),
            pltpu.SemaphoreType.DMA((9, 2)),
            pltpu.SemaphoreType.DMA((6,)),
        ],
        compiler_params=pltpu.CompilerParams(collective_id=0, has_side_effects=True, vmem_limit_bytes=grant),
        name="step",
    )(
        *(
            pltpu.with_memory_space_constraint(array, pltpu.HBM)
            for array in (
                positions, momenta, species.reshape(1, own),
                tile_a.reshape(1, slots), tile_b.reshape(1, slots),
            )
        ),
        tile_count,
    )
    return tuple(
        pl.pallas_call(
            finish_kernel,
            out_shape=(own_shape,) * 3,
            in_specs=[vmem] * 3,
            out_specs=(hbm,) * 3,
            scratch_shapes=[pltpu.SemaphoreType.DMA((3,))],
            compiler_params=pltpu.CompilerParams(vmem_limit_bytes=grant),
            name="finish",
        )(*outs)
    )


def solution(mesh):
    in_specs = (
        P(None, ("row", "col")),
        P(None, ("row", "col")),
        P(("row", "col")),
        P("row", "col", None),
        P("row", "col", None),
        P("row", "col"),
    )
    out_specs = (P(None, ("row", "col")), P(None, ("row", "col")), P(None, ("row", "col")))
    body = functools.partial(per_device, mesh.shape["row"], mesh.shape["col"])
    return jax.shard_map(body, mesh=mesh, in_specs=in_specs, out_specs=out_specs, check_vma=False)
```

```python
import functools
import math

import jax
import jax.numpy as jnp
from jax import lax
from jax.experimental import pallas as pl
from jax.experimental.pallas import tpu as pltpu
from jax.sharding import PartitionSpec as P

SOFTENING = 0.25
GRAVITY = 0.5
LIGHT_CHARGE = 1.0
HEAVY_CHARGE = 2.5
HALF_STEP = 0.1
TIME_STEP = 0.2
tile_width = 128
scale = 1.0 / math.log(2.0)
middle = 2.0
depth = 32
longest = 256
ahead = 8
grant = 48 * 2**20
MESH = pl.DeviceIdType.MESH
f32, bf16 = jnp.float32, jnp.bfloat16


def far_first(axes, name):
    me, size = lax.axis_index(name), axes[name]
    order = []
    for index in range(size - 1):
        down = size - 1 - index
        down = down - jnp.where(down <= me, 1, 0)
        up = index + jnp.where(index >= me, 1, 0)
        order.append({name: jnp.where(2 * me < size, down, up)})
    return order


def remote(source, target, sems, peer):
    return pltpu.make_async_remote_copy(
        src_ref=source,
        dst_ref=target,
        send_sem=sems.at[0],
        recv_sem=sems.at[1],
        device_id=peer,
        device_id_type=MESH,
    )


def await_bytes(region, sem):
    pltpu.make_async_copy(region, region, sem).wait()


def charge_of(species):
    return jnp.where(species == 1, HEAVY_CHARGE, LIGHT_CHARGE).astype(f32)


def pieces(value, number):
    parts = []
    for _ in range(number - 1):
        part = value.astype(bf16).astype(f32)
        parts.append(part)
        value = value - part
    parts.append(value.astype(bf16).astype(f32))
    return parts


pairs_of_pieces = ((0, 0), (0, 1), (1, 0), (0, 2), (2, 0), (1, 1))


def component(ref, start, index, count):
    return ref[pl.ds(start + index, count, stride=4), :]


def table_of(table, tile):
    rows, tiles, lanes = table.shape
    return table.reshape(rows * tiles, lanes)[pl.ds(tile, rows, stride=tiles), :]


def prepare_near(rows, base, near_f, near):
    tiles = near.shape[0]
    for start in range(0, tiles, 8):
        here = pl.ds(start, 8)
        square = 0.0
        for axis in range(3):
            value = (component(rows, base + 4 * start, axis, 8) - middle) * scale
            square = square + value * value
            split = pieces(value, 3)
            for row, (left, _) in enumerate(pairs_of_pieces):
                near_f[6 * axis + row, here, :] = -2.0 * split[left]
        for row, piece in enumerate(pieces(square, 3)):
            near_f[18 + row, here, :] = piece
    for tile in range(tiles):
        single = table_of(near_f, tile).astype(bf16)
        near[tile, :, :tile_width] = single
        near[tile, :, tile_width:] = -single


def prepare_far(cols, base, far_f, far, load_f, load):
    tiles = far.shape[0]
    for start in range(0, tiles, 8):
        here = pl.ds(start, 8)
        charge = component(cols, base + 4 * start, 3, 8)
        square = SOFTENING * scale * scale
        for axis in range(3):
            value = (component(cols, base + 4 * start, axis, 8) - middle) * scale
            square = square + value * value
            split = pieces(value, 3)
            for row, (_, right) in enumerate(pairs_of_pieces):
                far_f[6 * axis + row, here, :] = split[right]
            for row, piece in enumerate(pieces(charge * value, 2)):
                load_f[4 * row + axis, here, :] = piece
        load_f[3, here, :] = charge
        for row, piece in enumerate(pieces(square, 3)):
            far_f[21 + row, here, :] = piece
    for tile in range(tiles):
        far[tile] = table_of(far_f, tile).T.astype(bf16)
        single = table_of(load_f, tile).astype(bf16)
        load[tile, :, :tile_width] = single
        load[tile, :, tile_width:] = single


def visit_pairs(firsts, seconds, near, far, load, terms):
    slots = firsts.shape[1]
    unroll = math.gcd(slots, longest)

    def squares(slot):
        both = jnp.dot(far[seconds[0, slot]], near[firsts[0, slot]], preferred_element_type=f32)
        return both[:, :tile_width], both[:, tile_width:]

    def visit(step, carry):
        start = step * unroll
        ready = [squares(start + index) for index in range(ahead)]
        for index in range(unroll):
            slot = start + index
            square, negative = ready[index]
            if index + ahead < unroll:
                ready.append(squares(slot + ahead))
            inverse = lax.rsqrt(square)
            decay = jnp.exp2(negative * inverse)
            weight = decay * (inverse * inverse) * (inverse + 1.0 / scale)
            high = weight.astype(bf16)
            low = (weight - high.astype(f32)).astype(bf16)
            both = jnp.concatenate([high, low], axis=0)
            term = jnp.dot(load[seconds[0, slot]], both, preferred_element_type=f32)
            terms[pl.ds(pl.multiple_of(8 * slot, 8), 8), :] = term[:8]
        return carry

    if slots == unroll:
        visit(0, 0)
    else:
        lax.fori_loop(0, slots // unroll, visit, 0)


def combine(chosen, terms, partial, base):
    slots = chosen.shape[1]
    tiles = chosen.shape[0]

    def row(index):
        return terms[pl.ds(index, slots, stride=8), :]

    for part in range(4):
        value = row(part) if part == 3 else row(part) + row(4 + part)
        high = value.astype(bf16)
        low = (value - high.astype(f32)).astype(bf16)
        both = jnp.dot(chosen, jnp.concatenate([high, low], axis=1), preferred_element_type=f32)
        partial[pl.ds(base + part, tiles, stride=4), :] = both[:, :tile_width] + both[:, tile_width:]


def tiled(target, places, last, tiles):
    for tile in range(tiles):
        lanes = slice(tile * tile_width, (tile + 1) * tile_width)
        target[4 * tile : 4 * tile + 3, :] = places[:, lanes]
        target[4 * tile + 3 : 4 * tile + 4, :] = last[:, lanes]


def untiled(block, first, count, tiles):
    return jnp.concatenate([block[4 * tile + first : 4 * tile + first + count, :] for tile in range(tiles)], axis=1)


def terms_of(places, charge):
    third = lax.broadcasted_iota(jnp.int32, places.shape, 0) == 2
    return charge * (scale * scale), (places - middle) * scale, jnp.where(third, -GRAVITY * charge, 0.0)


def force_of(total, known, tiles):
    factor, places, weight = known
    return factor * (places * untiled(total, 3, 1, tiles) - untiled(total, 0, 3, tiles)) + weight


def step_kernel(
    axes, tiles, pos_hbm, mom_hbm, spec_hbm, first_hbm, second_hbm, count,
    moved_ref, ahead_ref, end_ref,
    spec_ref, first_ref, firsts, seconds,
    packed, twin_packed, twin_momenta, kicked, rows, cols, partial, arrived,
    near_f, near, far_f, far, load_f, load, terms, chosen,
    sems, fetch_sems,
):
    my_row, my_col = lax.axis_index("row"), lax.axis_index("col")
    col_count, row_count = axes["col"], axes["row"]
    across_col, across_row = far_first(axes, "col"), far_first(axes, "row")
    odd = lax.rem(my_row, 2)
    twin = my_row + 1 - 2 * odd
    across_twin = [{"row": twin, "col": peer["col"]} for peer in across_col] + [{"row": twin, "col": my_col}]
    height = 4 * tiles
    row_a, col_a, momenta_sems, sum_own, sum_twin, row_b, col_b, kick_sems, sum_b = (sems.at[which] for which in range(9))
    barrier = pltpu.get_barrier_semaphore()
    everyone = across_col + across_row
    for peer in everyone:
        pl.semaphore_signal(barrier, inc=1, device_id=peer, device_id_type=MESH)
    moves = (
        (pos_hbm, moved_ref), (spec_hbm, spec_ref), (mom_hbm, ahead_ref), (second_hbm, seconds), (first_hbm, firsts),
        (first_hbm, first_ref),
    )
    fetches = [pltpu.make_async_copy(source, target, fetch_sems.at[which]) for which, (source, target) in enumerate(moves)]
    for fetch in fetches:
        fetch.start()
    for fetch in fetches[:2]:
        fetch.wait()

    def block(size, turn, index):
        return pl.ds(pl.multiple_of((turn * size + index) * height, height), height)

    def several(count):
        return pl.ds(0, count * height)

    def send_packed(source, turn, row_targets, level, row_sems, col_sems):
        for peer in row_targets:
            remote(source, rows.at[block(col_count, turn, my_col)], row_sems, peer).start()
        for peer in across_row:
            remote(source, cols.at[block(row_count, turn, level)], col_sems, peer).start()

    def first_gather():
        send_packed(packed.at[0], 0, across_col, my_row, row_a, col_a)
        rows[block(col_count, 0, my_col)] = packed[0]
        cols[block(row_count, 0, my_row)] = packed[0]
        near_f[21:24] = jnp.ones((3,) + near_f.shape[1:], f32)
        near_f[24:] = jnp.zeros((depth - 24,) + near_f.shape[1:], f32)
        far_f[18:21] = jnp.ones((3,) + far_f.shape[1:], f32)
        far_f[24:] = jnp.zeros((depth - 24,) + far_f.shape[1:], f32)
        load_f[...] = jnp.zeros_like(load_f)
        for fetch in fetches[2:]:
            fetch.wait()

        @pl.when(odd == 0)
        def lend_momenta():
            tiled(kicked, ahead_ref[...], jnp.zeros((1, ahead_ref.shape[1]), f32), tiles)
            remote(kicked, twin_momenta, momenta_sems, across_twin[-1]).start()

        tile = lax.broadcasted_iota(jnp.int32, chosen.shape, 0)
        slot = lax.broadcasted_iota(jnp.int32, chosen.shape, 1)
        live = (tile == first_ref[...]) & (slot < count[0, 0])
        chosen[...] = jnp.where(live, 1.0, 0.0).astype(bf16)

    tiled(packed.at[0], moved_ref[...], charge_of(spec_ref[...]), tiles)
    pl.semaphore_wait(barrier, len(everyone))

    def on(turn, wanted, parity=None):
        return turn == wanted if parity is None else (turn == wanted) & (odd == parity)

    def kick(start, known, places, momenta, rate):
        half = momenta + HALF_STEP * force_of(added(start), known, tiles)
        return half, places + rate * half

    def added(start):
        total = arrived[block(col_count, start, 0)]
        for index in range(1, col_count):
            total = total + arrived[block(col_count, start, index)]
        return total

    def evaluate(turn, carry):
        pl.when(on(turn, 0))(first_gather)
        for wanted, parity, number in ((0, None, row_count - 1), (1, 0, row_count), (1, 1, row_count - 2)):
            @pl.when(on(turn, wanted, parity))
            def columns_arrive():
                await_bytes(cols.at[several(number)], (col_b if wanted else col_a).at[1])
        base, col_base = turn * col_count * height, turn * row_count * height
        prepare_far(cols, col_base, far_f, far, load_f, load)
        for wanted, parity, number in ((0, None, col_count - 1), (1, 0, col_count), (1, 1, col_count - 1)):
            @pl.when(on(turn, wanted, parity))
            def rows_arrive():
                await_bytes(rows.at[several(number)], (row_b if wanted else row_a).at[1])
        prepare_near(rows, base, near_f, near)
        visit_pairs(firsts, seconds, near, far, load, terms)
        combine(chosen[...], terms, partial, base)

        def send_partial(peer, target, pair):
            source = partial.at[block(col_count, turn, peer["col"])]
            remote(source, arrived.at[block(col_count, target, my_col)], pair, peer).start()

        @pl.when(on(turn, 0, 0))
        def lend_sums():
            for peer in across_twin:
                send_partial(peer, 1, sum_twin)
            await_bytes(kicked, momenta_sems.at[0])
            await_bytes(partial.at[several(col_count)], sum_twin.at[0])

        @pl.when(on(turn, 0, 1))
        def move():
            for peer in across_col:
                send_partial(peer, 0, sum_own)
            arrived[block(col_count, 0, my_col)] = partial[block(col_count, turn, my_col)]
            charge, places, momenta = charge_of(spec_ref[...]), moved_ref[...], ahead_ref[...]
            known, rate = terms_of(places, charge), TIME_STEP / charge
            await_bytes(arrived.at[several(col_count - 1)], sum_own.at[1])
            half, moved = kick(0, known, places, momenta, rate)
            tiled(packed.at[1], moved, charge, tiles)
            send_packed(packed.at[1], 1, across_col, my_row, row_b, col_b)
            ahead_ref[...] = half
            moved_ref[...] = moved
            await_bytes(twin_momenta, momenta_sems.at[1])
            other = cols[block(row_count, 0, twin)]
            charge, places = untiled(other, 3, 1, tiles), untiled(other, 0, 3, tiles)
            momenta = untiled(twin_momenta[...], 0, 3, tiles)
            known, rate = terms_of(places, charge), TIME_STEP / charge
            await_bytes(arrived.at[several(col_count)], sum_twin.at[1])
            half, moved = kick(1, known, places, momenta, rate)
            tiled(twin_packed, moved, charge, tiles)
            send_packed(twin_packed, 1, across_twin, twin, row_b, col_b)
            cols[block(row_count, 1, twin)] = twin_packed[...]
            tiled(kicked, half, charge, tiles)
            remote(kicked, twin_momenta, kick_sems, across_twin[-1]).start()
            rows[block(col_count, 1, my_col)] = packed[1]
            cols[block(row_count, 1, my_row)] = packed[1]
            await_bytes(partial.at[several(col_count - 1)], sum_own.at[0])

        @pl.when(on(turn, 1))
        def end():
            for peer in across_col:
                send_partial(peer, 2, sum_b)
            arrived[block(col_count, 2, my_col)] = partial[block(col_count, turn, my_col)]

            @pl.when(odd == 0)
            def take_back():
                await_bytes(twin_momenta, kick_sems.at[1])
                moved_ref[...] = untiled(rows[block(col_count, 1, my_col)], 0, 3, tiles)
                ahead_ref[...] = untiled(twin_momenta[...], 0, 3, tiles)

            @pl.when(odd == 1)
            def sent():
                await_bytes(kicked, kick_sems.at[0])
                await_bytes(rows.at[several(2 * col_count - 1)], row_b.at[0])
                await_bytes(cols.at[several(2 * row_count - 2)], col_b.at[0])

            known, momenta = terms_of(moved_ref[...], charge_of(spec_ref[...])), ahead_ref[...]
            await_bytes(arrived.at[several(col_count - 1)], sum_b.at[1])
            force = force_of(added(2), known, tiles)
            ahead_ref[...] = momenta + HALF_STEP * force
            end_ref[...] = force
            await_bytes(rows.at[several(col_count - 1)], row_a.at[0])
            await_bytes(cols.at[several(row_count - 1)], col_a.at[0])
            await_bytes(partial.at[several(col_count - 1)], sum_b.at[0])

        return carry

    lax.fori_loop(0, 2, evaluate, 0)


def finish_kernel(moved_ref, ahead_ref, end_ref, trial_ref, momenta_ref, force_ref, sems):
    moves = ((moved_ref, trial_ref), (ahead_ref, momenta_ref), (end_ref, force_ref))
    copies = [pltpu.make_async_copy(source, target, sems.at[which]) for which, (source, target) in enumerate(moves)]
    for copy in copies:
        copy.start()
    for copy in copies:
        copy.wait()


def per_device(row_count, col_count, positions, momenta, species, tile_a, tile_b, tile_count):
    own = positions.shape[1]
    tiles = own // tile_width
    axes = {"col": col_count, "row": row_count}
    vmem = pl.BlockSpec(memory_space=pltpu.VMEM)
    hbm = pl.BlockSpec(memory_space=pltpu.HBM)
    slots = tile_a.shape[-1]
    near_count, far_count = col_count * tiles, row_count * tiles
    own_shape = jax.ShapeDtypeStruct((3, own), f32)
    tiled_block = pltpu.VMEM((4 * tiles, tile_width), f32)
    rows = pltpu.VMEM((2 * near_count * 4, tile_width), f32)
    cols = pltpu.VMEM((2 * far_count * 4, tile_width), f32)
    outs = pl.pallas_call(
        functools.partial(step_kernel, axes, tiles),
        out_shape=(own_shape,) * 3,
        in_specs=[hbm] * 5 + [pl.BlockSpec(memory_space=pltpu.SMEM)],
        out_specs=(vmem,) * 3,
        scratch_shapes=[
            pltpu.VMEM((1, own), jnp.int32), pltpu.VMEM((1, slots), jnp.int32),
            pltpu.SMEM((1, slots), jnp.int32), pltpu.SMEM((1, slots), jnp.int32),
            pltpu.VMEM((2, 4 * tiles, tile_width), f32), tiled_block, tiled_block, tiled_block,
            rows, cols, rows, pltpu.VMEM((3 * near_count * 4, tile_width), f32),
            pltpu.VMEM((depth, near_count, tile_width), f32),
            pltpu.VMEM((near_count, depth, 2 * tile_width), bf16),
            pltpu.VMEM((depth, far_count, tile_width), f32),
            pltpu.VMEM((far_count, tile_width, depth), bf16),
            pltpu.VMEM((16, far_count, tile_width), f32),
            pltpu.VMEM((far_count, 16, 2 * tile_width), bf16),
            pltpu.VMEM((8 * slots, tile_width), f32),
            pltpu.VMEM((near_count, slots), bf16),
            pltpu.SemaphoreType.DMA((9, 2)),
            pltpu.SemaphoreType.DMA((6,)),
        ],
        compiler_params=pltpu.CompilerParams(collective_id=0, has_side_effects=True, vmem_limit_bytes=grant),
        name="step",
    )(
        *(
            pltpu.with_memory_space_constraint(array, pltpu.HBM)
            for array in (
                positions, momenta, species.reshape(1, own),
                tile_a.reshape(1, slots), tile_b.reshape(1, slots),
            )
        ),
        tile_count,
    )
    return tuple(
        pl.pallas_call(
            finish_kernel,
            out_shape=(own_shape,) * 3,
            in_specs=[vmem] * 3,
            out_specs=(hbm,) * 3,
            scratch_shapes=[pltpu.SemaphoreType.DMA((3,))],
            compiler_params=pltpu.CompilerParams(vmem_limit_bytes=grant),
            name="finish",
        )(*outs)
    )


def solution(mesh):
    in_specs = (
        P(None, ("row", "col")),
        P(None, ("row", "col")),
        P(("row", "col")),
        P("row", "col", None),
        P("row", "col", None),
        P("row", "col"),
    )
    out_specs = (P(None, ("row", "col")), P(None, ("row", "col")), P(None, ("row", "col")))
    body = functools.partial(per_device, mesh.shape["row"], mesh.shape["col"])
    return jax.shard_map(body, mesh=mesh, in_specs=in_specs, out_specs=out_specs, check_vma=False)
```
